32 devices in a mesh: dp: 16 (over z, y, x), tensor: 2 (over core).
Axes of the slice: x: 2, y: 2, z: 4, core: 2. Of those that a mesh axis runs over, the one named last changes fastest.
Arguments:
- block_in: bfloat16 [32768, 1536], P('dp'), may hold values from -30 to 30
- prefix_len: int32 [32], P('dp'), may hold values from 0 to 1024
- out_grad: bfloat16 [32768, 1536], P('dp'), may hold values from -6 to 6
- step_count: int32 [1], replicated, may hold values from 2 to 20
- q_weight: float32 [1536, 1536], P('dp', 'tensor'), may hold values from -0.15625 to 0.15625
- key_matrix: float32 [1536, 768], P('dp', 'tensor'), may hold values from -0.15625 to 0.15625
- value_matrix: float32 [1536, 768], P('dp', 'tensor'), may hold values from -0.15625 to 0.15625
- o_weight: float32 [1536, 1536], P('dp', 'tensor'), may hold values from -2.5 to 2.5
- gate_weight: float32 [1536, 4096], P('dp', 'tensor'), may hold values from -0.15625 to 0.15625
- up_weight: float32 [1536, 4096], P('dp', 'tensor'), may hold values from -0.15625 to 0.15625
- down_weight: float32 [1536, 4096], P('dp', 'tensor'), may hold values from -0.1875 to 0.1875
- norm_gains: float32 [2, 1536], replicated, may hold values from 0.25 to 1.75
- query_mean_moment: float32 [1536, 1536], P('dp', 'tensor'), may hold values from -0.00018310547 to 0.00018310547
- key_mean_moment: float32 [1536, 768], P('dp', 'tensor'), may hold values from -0.00024414062 to 0.00024414062
- value_mean_moment: float32 [1536, 768], P('dp', 'tensor'), may hold values from -0.00024414062 to 0.00024414062
- output_mean_moment: float32 [1536, 1536], P('dp', 'tensor'), may hold values from -1.335144e-05 to 1.335144e-05
- gate_mean_moment: float32 [1536, 4096], P('dp', 'tensor'), may hold values from -9.1552734e-05 to 9.1552734e-05
- up_mean_moment: float32 [1536, 4096], P('dp', 'tensor'), may hold values from -0.00010681152 to 0.00010681152
- down_mean_moment: float32 [1536, 4096], P('dp', 'tensor'), may hold values from -7.6293945e-05 to 7.6293945e-05
- gains_mean_moment: float32 [2, 1536], P(None, 'dp'), may hold values from -0.00024414062 to 0.00024414062
- q_second: float32 [1536, 1536], P('dp', 'tensor'), may hold values from 4.571947e-09 to 1.8287787e-08
- key_square_moment: float32 [1536, 768], P('dp', 'tensor'), may hold values from 9.321445e-09 to 3.7374555e-08
- value_square_moment: float32 [1536, 768], P('dp', 'tensor'), may hold values from 9.321445e-09 to 3.7374555e-08
- o_second: float32 [1536, 1536], P('dp', 'tensor'), may hold values from 2.3525551e-11 to 9.321445e-11
- gate_second: float32 [1536, 4096], P('dp', 'tensor'), may hold values from 1.0519916e-09 to 4.2035277e-09
- up_second: float32 [1536, 4096], P('dp', 'tensor'), may hold values from 1.2384205e-09 to 4.953682e-09
- down_second: float32 [1536, 4096], P('dp', 'tensor'), may hold values from 8.3893004e-10 to 3.3645977e-09
- gains_second: float32 [2, 1536], P(None, 'dp'), may hold values from 7.102053e-09 to 4.4387832e-08
Outputs:
- block_out: bfloat16 [32768, 1536], P('dp')
- in_grad: float32 [32768, 1536], P('dp')
- grad_norm: float32 [1], replicated
- new_q_weight: float32 [1536, 1536], P('dp', 'tensor')
- new_k_weight: float32 [1536, 768], P('dp', 'tensor')
- new_v_weight: float32 [1536, 768], P('dp', 'tensor')
- new_o_weight: float32 [1536, 1536], P('dp', 'tensor')
- new_gate_weight: float32 [1536, 4096], P('dp', 'tensor')
- new_up_weight: float32 [1536, 4096], P('dp', 'tensor')
- new_down_weight: float32 [1536, 4096], P('dp', 'tensor')
- new_norm_gains: float32 [2, 1536], P(None, 'dp')
- new_q_first: float32 [1536, 1536], P('dp', 'tensor')
- new_k_first: float32 [1536, 768], P('dp', 'tensor')
- new_v_first: float32 [1536, 768], P('dp', 'tensor')
- new_o_first: float32 [1536, 1536], P('dp', 'tensor')
- new_gate_first: float32 [1536, 4096], P('dp', 'tensor')
- new_up_first: float32 [1536, 4096], P('dp', 'tensor')
- new_down_first: float32 [1536, 4096], P('dp', 'tensor')
- new_gains_first: float32 [2, 1536], P(None, 'dp')
- new_q_second: float32 [1536, 1536], P('dp', 'tensor')
- new_k_second: float32 [1536, 768], P('dp', 'tensor')
- new_v_second: float32 [1536, 768], P('dp', 'tensor')
- new_o_second: float32 [1536, 1536], P('dp', 'tensor')
- new_gate_second: float32 [1536, 4096], P('dp', 'tensor')
- new_up_second: float32 [1536, 4096], P('dp', 'tensor')
- new_down_second: float32 [1536, 4096], P('dp', 'tensor')
- new_gains_second: float32 [2, 1536], P(None, 'dp')
The draws below stay inside these ranges and needn't reach their ends.
All inputs are finite; a program needn't handle non-finite values.
Results may differ from the reference program's by a relative error of at most 0.018.
Values may be sent and summed in bfloat16 or wider, within the bound.
A program may use at most 320 MiB of HBM per device.

```python
import math
import jax
import jax.numpy as jnp
from jax import lax

MODEL_WIDTH = 1536
QUERY_HEADS = 16
KEY_VALUE_HEADS = 8
HEAD_WIDTH = 96
FEEDFORWARD_UNITS = 4096
SEQUENCE_LENGTH = 1024
QUERY_BLOCK_ROWS = 512
SEQ_DEV = 2
TOK_DEV = 2048
SEQS = 32
TOKENS = 32768
N_TENSOR = 2


def draw_block_in(key, part):
    key_one, key_two, key_three = jax.random.split(key, 3)
    columns = jnp.exp(jax.random.uniform(key_three, (1, MODEL_WIDTH), jnp.float32, math.log(0.4), math.log(2.5)))
    entries = jnp.clip(jax.random.normal(key_one, (TOKENS, MODEL_WIDTH), jnp.float32), -4.0, 4.0)
    row_scales = jnp.exp(jax.random.uniform(key_two, (TOKENS, 1), jnp.float32, math.log(0.3), math.log(3.0)))
    return (entries * row_scales * columns).astype(jnp.bfloat16)


def touch_ends(values, stream_key, least, high):
    extent = values.shape
    spot = [jax.random.randint(jax.random.fold_in(stream_key, axis), (), 0, extent[axis]) for axis in range(len(extent))]
    values = values.at[tuple(spot)].set(least)
    longest = extent.index(max(extent))
    spot[longest] = (spot[longest] + 1) % extent[longest]
    return values.at[tuple(spot)].set(high)


def level_of(key, dims, cuts, least, high):
    loudness = 1.0
    for axis_at, shards_of in cuts:
        steps = jax.random.uniform(jax.random.fold_in(jax.random.fold_in(key, 6), axis_at), (shards_of,), jnp.float32, least / len(cuts), high / len(cuts))
        loudness = loudness * jnp.repeat(jnp.exp(steps), dims[axis_at] // shards_of).reshape((-1,) + (1,) * (len(dims) - 1 - axis_at))
    return loudness


def scatter_about(rng, shape, deviation, limit, cuts=(), kind=jnp.bfloat16):
    factor_of = level_of(rng, shape, cuts, -0.22, 0.18) if cuts else 1.0
    values = jax.random.normal(rng, shape, jnp.float32) * deviation * factor_of
    return jnp.minimum(jnp.maximum(values, -limit), limit).astype(kind)


def setup_inputs(seed: int = 0) -> dict:
    splits = jax.random.split(jax.random.key(seed), 29)
    return {
        "block_in": draw_block_in(jax.random.fold_in(splits[28], 71), 0),
        "prefix_len": touch_ends(jax.random.randint(splits[1], (SEQS,), 0, SEQUENCE_LENGTH + 1), jax.random.fold_in(splits[1], 1), 0, SEQUENCE_LENGTH).astype(jnp.int32),
        "out_grad": scatter_about(splits[2], (TOKENS, MODEL_WIDTH), 1.0, 6.0, ((0, 16),)),
        "step_count": jax.random.randint(splits[3], (1,), 2, 21).astype(jnp.int32),
        "q_weight": scatter_about(splits[4], (MODEL_WIDTH, QUERY_HEADS * HEAD_WIDTH), MODEL_WIDTH ** -0.5, 0.15625, ((0, 16), (1, 2)), jnp.float32),
        "key_matrix": scatter_about(splits[5], (MODEL_WIDTH, KEY_VALUE_HEADS * HEAD_WIDTH), MODEL_WIDTH ** -0.5, 0.15625, ((0, 16), (1, 2)), jnp.float32),
        "value_matrix": scatter_about(splits[6], (MODEL_WIDTH, KEY_VALUE_HEADS * HEAD_WIDTH), MODEL_WIDTH ** -0.5, 0.15625, ((0, 16), (1, 2)), jnp.float32),
        "o_weight": scatter_about(splits[7], (MODEL_WIDTH, QUERY_HEADS * HEAD_WIDTH), (max(1, QUERY_HEADS * HEAD_WIDTH * 4 // SEQUENCE_LENGTH)) ** -0.5, 2.5, ((0, 16), (1, 2)), jnp.float32),
        "gate_weight": scatter_about(splits[8], (MODEL_WIDTH, FEEDFORWARD_UNITS), MODEL_WIDTH ** -0.5, 0.15625, ((0, 16), (1, 2)), jnp.float32),
        "up_weight": scatter_about(splits[9], (MODEL_WIDTH, FEEDFORWARD_UNITS), MODEL_WIDTH ** -0.5, 0.15625, ((0, 16), (1, 2)), jnp.float32),
        "down_weight": scatter_about(splits[10], (MODEL_WIDTH, FEEDFORWARD_UNITS), (FEEDFORWARD_UNITS // 4) ** -0.5, 0.1875, ((0, 16), (1, 2)), jnp.float32),
        "norm_gains": jnp.clip(1.0 + 0.15 * jax.random.normal(splits[11], (2, MODEL_WIDTH), jnp.float32), 0.25, 1.75),
        "query_mean_moment": scatter_about(splits[12], (MODEL_WIDTH, QUERY_HEADS * HEAD_WIDTH), (155 * (10000 * MODEL_WIDTH * (197 * QUERY_HEADS * HEAD_WIDTH + 800 * KEY_VALUE_HEADS * HEAD_WIDTH + 134 * FEEDFORWARD_UNITS + 856)) ** -0.5), 0.00018310547, ((0, 16), (1, 2)), jnp.float32),
        "key_mean_moment": scatter_about(splits[13], (MODEL_WIDTH, KEY_VALUE_HEADS * HEAD_WIDTH), (222 * (10000 * MODEL_WIDTH * (197 * QUERY_HEADS * HEAD_WIDTH + 800 * KEY_VALUE_HEADS * HEAD_WIDTH + 134 * FEEDFORWARD_UNITS + 856)) ** -0.5), 0.00024414062, ((0, 16), (1, 2)), jnp.float32),
        "value_mean_moment": scatter_about(splits[14], (MODEL_WIDTH, KEY_VALUE_HEADS * HEAD_WIDTH), (222 * (10000 * MODEL_WIDTH * (197 * QUERY_HEADS * HEAD_WIDTH + 800 * KEY_VALUE_HEADS * HEAD_WIDTH + 134 * FEEDFORWARD_UNITS + 856)) ** -0.5), 0.00024414062, ((0, 16), (1, 2)), jnp.float32),
        "output_mean_moment": scatter_about(splits[15], (MODEL_WIDTH, QUERY_HEADS * HEAD_WIDTH), (111 * (1000000 * MODEL_WIDTH * (197 * QUERY_HEADS * HEAD_WIDTH + 800 * KEY_VALUE_HEADS * HEAD_WIDTH + 134 * FEEDFORWARD_UNITS + 856)) ** -0.5), 1.33514404296875e-05, ((0, 16), (1, 2)), jnp.float32),
        "gate_mean_moment": scatter_about(splits[16], (MODEL_WIDTH, FEEDFORWARD_UNITS), (744 * (1000000 * MODEL_WIDTH * (197 * QUERY_HEADS * HEAD_WIDTH + 800 * KEY_VALUE_HEADS * HEAD_WIDTH + 134 * FEEDFORWARD_UNITS + 856)) ** -0.5), 9.1552734375e-05, ((0, 16), (1, 2)), jnp.float32),
        "up_mean_moment": scatter_about(splits[17], (MODEL_WIDTH, FEEDFORWARD_UNITS), (81 * (10000 * MODEL_WIDTH * (197 * QUERY_HEADS * HEAD_WIDTH + 800 * KEY_VALUE_HEADS * HEAD_WIDTH + 134 * FEEDFORWARD_UNITS + 856)) ** -0.5), 0.00010681152, ((0, 16), (1, 2)), jnp.float32),
        "down_mean_moment": scatter_about(splits[18], (MODEL_WIDTH, FEEDFORWARD_UNITS), (667 * (1000000 * MODEL_WIDTH * (197 * QUERY_HEADS * HEAD_WIDTH + 800 * KEY_VALUE_HEADS * HEAD_WIDTH + 134 * FEEDFORWARD_UNITS + 856)) ** -0.5), 7.62939453125e-05, ((0, 16), (1, 2)), jnp.float32),
        "gains_mean_moment": scatter_about(splits[19], (2, MODEL_WIDTH), (22 * (100 * MODEL_WIDTH * (197 * QUERY_HEADS * HEAD_WIDTH + 800 * KEY_VALUE_HEADS * HEAD_WIDTH + 134 * FEEDFORWARD_UNITS + 856)) ** -0.5), 0.00024414062, ((1, 16),), jnp.float32),
        "q_second": jnp.clip(jnp.exp(math.log(1.8287787284521073e-08) - 1.3862944 * jax.random.uniform(splits[20], (MODEL_WIDTH, QUERY_HEADS * HEAD_WIDTH), jnp.float32) ** level_of(splits[20], (MODEL_WIDTH, QUERY_HEADS * HEAD_WIDTH), ((0, 16), (1, 2)), -0.2, 0.2)), 4.571946821130268e-09, 1.8287787284521073e-08),
        "key_square_moment": jnp.clip(jnp.exp(math.log(3.737455500640863e-08) - 1.3886725 * jax.random.uniform(splits[21], (MODEL_WIDTH, KEY_VALUE_HEADS * HEAD_WIDTH), jnp.float32) ** level_of(splits[21], (MODEL_WIDTH, KEY_VALUE_HEADS * HEAD_WIDTH), ((0, 16), (1, 2)), -0.2, 0.2)), 9.32144494925069e-09, 3.737455500640863e-08),
        "value_square_moment": jnp.clip(jnp.exp(math.log(3.737455500640863e-08) - 1.3886725 * jax.random.uniform(splits[22], (MODEL_WIDTH, KEY_VALUE_HEADS * HEAD_WIDTH), jnp.float32) ** level_of(splits[22], (MODEL_WIDTH, KEY_VALUE_HEADS * HEAD_WIDTH), ((0, 16), (1, 2)), -0.2, 0.2)), 9.32144494925069e-09, 3.737455500640863e-08),
        "o_second": jnp.clip(jnp.exp(math.log(9.321445004761841e-11) - 1.37681563 * jax.random.uniform(splits[23], (MODEL_WIDTH, QUERY_HEADS * HEAD_WIDTH), jnp.float32) ** level_of(splits[23], (MODEL_WIDTH, QUERY_HEADS * HEAD_WIDTH), ((0, 16), (1, 2)), -0.2, 0.2)), 2.35255512986976e-11, 9.321445004761841e-11),
        "gate_second": jnp.clip(jnp.exp(math.log(4.203527748103397e-09) - 1.385239 * jax.random.uniform(splits[24], (MODEL_WIDTH, FEEDFORWARD_UNITS), jnp.float32) ** level_of(splits[24], (MODEL_WIDTH, FEEDFORWARD_UNITS), ((0, 16), (1, 2)), -0.2, 0.2)), 1.0519916049389622e-09, 4.203527748103397e-09),
        "up_second": jnp.clip(jnp.exp(math.log(4.9536819091144935e-09) - 1.3862944 * jax.random.uniform(splits[25], (MODEL_WIDTH, FEEDFORWARD_UNITS), jnp.float32) ** level_of(splits[25], (MODEL_WIDTH, FEEDFORWARD_UNITS), ((0, 16), (1, 2)), -0.2, 0.2)), 1.2384204772786234e-09, 4.9536819091144935e-09),
        "down_second": jnp.clip(jnp.exp(math.log(3.3645977115526193e-09) - 1.3889364 * jax.random.uniform(splits[26], (MODEL_WIDTH, FEEDFORWARD_UNITS), jnp.float32) ** level_of(splits[26], (MODEL_WIDTH, FEEDFORWARD_UNITS), ((0, 16), (1, 2)), -0.2, 0.2)), 8.389300365507779e-10, 3.3645977115526193e-09),
        "gains_second": jnp.clip(jnp.exp(math.log(4.43878320766089e-08) - 1.83258146 * jax.random.uniform(splits[27], (2, MODEL_WIDTH), jnp.float32) ** level_of(splits[27], (2, MODEL_WIDTH), ((1, 16),), -0.2, 0.2)), 7.102053167784561e-09, 4.43878320766089e-08),
    }


theta_base = 100000.0
norm_eps = 1e-05
beta_one = 0.9
beta_two = 0.95
adam_eps = 1e-08
decay_rate = 0.1
clip_limit = 1.0
neg_fill = -1e+30
matrix_rates = (0.08, 0.08, 0.08, 1.0, 0.08, 0.08, 0.1)
gain_rate = 1.0
highest = lax.Precision.HIGHEST

@jax.custom_vjp
def narrow_cast(v):
    return lax.optimization_barrier(v.astype(jnp.bfloat16)).astype(jnp.float32)

@jax.custom_vjp
def narrow_cast_backward(v):
    return v

def low_keep(v):
    return (narrow_cast(v), None)

def low_pass(kept, grad):
    return (grad,)

def back_keep(v):
    return (v, None)

def back_low(kept, grad):
    return (narrow_cast(grad),)
narrow_cast.defvjp(low_keep, low_pass)
narrow_cast_backward.defvjp(back_keep, back_low)

def rotary_tables(length, head_size):
    half_size = head_size // 2
    frequency = jnp.power(theta_base, -2.0 * jnp.arange(half_size, dtype=jnp.float32) / head_size)
    angles = jnp.arange(length, dtype=jnp.float32)[:, None] * frequency[None, :]
    cosine_values = jnp.cos(angles)
    sine_values = jnp.sin(angles)
    return (jnp.concatenate([cosine_values, cosine_values], 1)[:, None, :], jnp.concatenate([sine_values, sine_values], 1)[:, None, :])

def rotary_apply(values, cosine_values, sine_values):
    half_size = values.shape[-1] // 2
    turned = jnp.concatenate([-values[..., half_size:], values[..., :half_size]], -1)
    return values * cosine_values + turned * sine_values

def normalize(row_values):
    return row_values * lax.rsqrt(lax.optimization_barrier(jnp.mean(row_values * row_values, -1, keepdims=True)) + norm_eps)

def matrix_multiply(left_side, right_side):
    return jnp.dot(left_side, right_side, preferred_element_type=jnp.float32, precision=highest)

def split_product(left_side, weight_low):
    parts = left_side.reshape(left_side.shape[0], N_TENSOR, -1)
    pieces = weight_low.reshape(weight_low.shape[0], N_TENSOR, -1)
    return jnp.einsum('tnj,dnj->ntd', parts, pieces, precision=highest)

def attend_sequence(seq_item):
    query_rows_block, key_row_slice, value_row_slice, prefix = seq_item
    score_scale = 1.0 / math.sqrt(HEAD_WIDTH)
    block_list = SEQUENCE_LENGTH // QUERY_BLOCK_ROWS
    first_rows = jnp.arange(block_list, dtype=jnp.int32) * QUERY_BLOCK_ROWS
    query_block_list = query_rows_block.reshape(block_list, QUERY_BLOCK_ROWS, KEY_VALUE_HEADS, QUERY_HEADS // KEY_VALUE_HEADS, HEAD_WIDTH)

    def one_block(block_item):
        q_block, first_row = block_item
        raw_scores = narrow_cast_backward(jnp.einsum('qhgd,khd->hgqk', q_block, key_row_slice, precision=highest) * score_scale)
        query_places = first_row + lax.broadcasted_iota(jnp.int32, (QUERY_BLOCK_ROWS, SEQUENCE_LENGTH), 0)
        key_places = lax.broadcasted_iota(jnp.int32, (QUERY_BLOCK_ROWS, SEQUENCE_LENGTH), 1)
        scores = jnp.where((key_places <= query_places) | (key_places < prefix), raw_scores, neg_fill)
        row_peak = lax.optimization_barrier(jnp.max(scores, -1, keepdims=True))
        exponent = jnp.exp(scores - row_peak)
        probability = narrow_cast(exponent / lax.optimization_barrier(jnp.sum(exponent, -1, keepdims=True)))
        return jnp.einsum('hgqk,khd->qhgd', probability, value_row_slice, precision=highest)
    mixed_out = lax.map(jax.checkpoint(one_block), (query_block_list, first_rows))
    return mixed_out.reshape(SEQUENCE_LENGTH, QUERY_HEADS * HEAD_WIDTH)

def forward(params, row_values, prefixes):
    q_weight, key_matrix, value_matrix, o_weight, gate_weight, up_weight, down_weight, norm_gains = params
    q_low = narrow_cast(q_weight)
    key_weight_narrow = narrow_cast(key_matrix)
    value_weight_narrow = narrow_cast(value_matrix)
    o_low = narrow_cast(o_weight)
    gate_low = narrow_cast(gate_weight)
    up_low = narrow_cast(up_weight)
    down_low = narrow_cast(down_weight)
    row_count = row_values.shape[0]
    sequence_count = row_count // SEQUENCE_LENGTH
    cosine_values, sine_values = rotary_tables(SEQUENCE_LENGTH, HEAD_WIDTH)
    first_normed_input = narrow_cast(normalize(row_values) * norm_gains[0])
    query_rows_block = narrow_cast_backward(matrix_multiply(first_normed_input, q_low)).reshape(sequence_count, SEQUENCE_LENGTH, QUERY_HEADS, HEAD_WIDTH)
    key_row_slice = narrow_cast_backward(matrix_multiply(first_normed_input, key_weight_narrow)).reshape(sequence_count, SEQUENCE_LENGTH, KEY_VALUE_HEADS, HEAD_WIDTH)
    value_row_slice = narrow_cast(narrow_cast_backward(matrix_multiply(first_normed_input, value_weight_narrow))).reshape(sequence_count, SEQUENCE_LENGTH, KEY_VALUE_HEADS, HEAD_WIDTH)
    query_rows_block = narrow_cast(rotary_apply(query_rows_block, cosine_values, sine_values)).reshape(sequence_count, SEQUENCE_LENGTH, KEY_VALUE_HEADS, QUERY_HEADS // KEY_VALUE_HEADS, HEAD_WIDTH)
    key_row_slice = narrow_cast(rotary_apply(key_row_slice, cosine_values, sine_values))
    mixed_out = lax.map(attend_sequence, (query_rows_block, key_row_slice, value_row_slice, prefixes))
    mixed_out = narrow_cast(narrow_cast_backward(mixed_out.reshape(row_count, QUERY_HEADS * HEAD_WIDTH)))
    attn_out = narrow_cast_backward(lax.optimization_barrier(jnp.sum(narrow_cast(split_product(mixed_out, o_low)), 0)))
    middle = row_values + attn_out
    normed_two = narrow_cast(normalize(middle) * norm_gains[1])
    gate_value = narrow_cast_backward(matrix_multiply(normed_two, gate_low))
    up_value = narrow_cast_backward(matrix_multiply(normed_two, up_low))
    hidden = narrow_cast(gate_value * jax.nn.sigmoid(gate_value) * up_value)
    ffn_out = narrow_cast_backward(lax.optimization_barrier(jnp.sum(narrow_cast(split_product(hidden, down_low)), 0)))
    return middle + ffn_out

def adam_step(weight, gradient, first_moment, second_moment, rate, decay, factor, fix_one, fix_two):
    clipped = factor * gradient
    first_new = beta_one * first_moment + (1.0 - beta_one) * clipped
    second_new = beta_two * second_moment + (1.0 - beta_two) * clipped * clipped
    update = first_new / fix_one / (jnp.sqrt(second_new / fix_two) + adam_eps) + decay * weight
    return (weight - rate * update, first_new, second_new)

def reference(block_in, prefix_len, out_grad, step_count, q_weight, key_matrix, value_matrix, o_weight, gate_weight, up_weight, down_weight, norm_gains, query_mean_moment, key_mean_moment, value_mean_moment, output_mean_moment, gate_mean_moment, up_mean_moment, down_mean_moment, gains_mean_moment, q_second, key_square_moment, value_square_moment, o_second, gate_second, up_second, down_second, gains_second):
    params = (q_weight, key_matrix, value_matrix, o_weight, gate_weight, up_weight, down_weight, norm_gains)
    inputs = block_in.astype(jnp.float32).reshape(-1, TOK_DEV, MODEL_WIDTH)
    backs = out_grad.astype(jnp.float32).reshape(-1, TOK_DEV, MODEL_WIDTH)
    prefixes = prefix_len.reshape(-1, SEQ_DEV)

    def group_step(totals, group_item):
        row_values, back_rows, group_prefix = group_item
        result, pull = jax.vjp(lambda weights, inputs_now: forward(weights, inputs_now, group_prefix), params, row_values)
        weight_grads, row_grads = pull(back_rows)
        return (jax.tree.map(jnp.add, totals, weight_grads), (result.astype(jnp.bfloat16), row_grads))
    zeros_tree = jax.tree.map(jnp.zeros_like, params)
    totals, (outputs, in_grads) = lax.scan(group_step, zeros_tree, (inputs, backs, prefixes))
    grad_norm = jnp.sqrt(sum((jnp.sum(jnp.square(gradient)) for gradient in totals)))
    factor = jnp.minimum(1.0, clip_limit / grad_norm)
    step_float = step_count[0].astype(jnp.float32)
    fix_one = 1.0 - jnp.power(beta_one, step_float)
    fix_two = 1.0 - jnp.power(beta_two, step_float)
    firsts = (query_mean_moment, key_mean_moment, value_mean_moment, output_mean_moment, gate_mean_moment, up_mean_moment, down_mean_moment, gains_mean_moment)
    seconds = (q_second, key_square_moment, value_square_moment, o_second, gate_second, up_second, down_second, gains_second)
    rate_list = matrix_rates + (gain_rate,)
    decay_list = (decay_rate,) * 7 + (0.0,)
    new_weights, new_firsts, new_seconds = ([], [], [])
    for weight, gradient, first_moment, second_moment, rate, decay in zip(params, totals, firsts, seconds, rate_list, decay_list):
        weight_new, first_new, second_new = adam_step(weight, gradient, first_moment, second_moment, rate, decay, factor, fix_one, fix_two)
        new_weights.append(weight_new)
        new_firsts.append(first_new)
        new_seconds.append(second_new)
    return (outputs.reshape(-1, MODEL_WIDTH), in_grads.reshape(-1, MODEL_WIDTH), grad_norm.reshape(1), new_weights[0], new_weights[1], new_weights[2], new_weights[3], new_weights[4], new_weights[5], new_weights[6], new_weights[7], new_firsts[0], new_firsts[1], new_firsts[2], new_firsts[3], new_firsts[4], new_firsts[5], new_firsts[6], new_firsts[7], new_seconds[0], new_seconds[1], new_seconds[2], new_seconds[3], new_seconds[4], new_seconds[5], new_seconds[6], new_seconds[7])
```

```python
import functools
import math

import jax
import jax.numpy as jnp
from jax import lax
from jax.experimental import pallas as pl
from jax.experimental.pallas import tpu as pltpu
from jax.sharding import PartitionSpec as P

HEAD_WIDTH = 96
GROUP_WIDTH = 2
SEQUENCE_LENGTH = 1024
QUERY_CHUNK = 512
VMEM_BYTES = 58 * 2**20
LOG2_E = 1.4426950408889634
SCORE_SCALE = 1.0 / math.sqrt(HEAD_WIDTH)

theta_base = 100000.0
norm_eps = 1e-05
beta_one = 0.9
beta_two = 0.95
adam_eps = 1e-08
decay_rate = 0.1
clip_limit = 1.0
neg_fill = -1e30
matrix_rates = (0.08, 0.08, 0.08, 1.0, 0.08, 0.08, 0.1)
gain_rate = 1.0

BF16 = jnp.bfloat16
F32 = jnp.float32
ANYWHERE = pl.BlockSpec(memory_space=pl.ANY)
MESH_ID = pl.DeviceIdType.MESH
GATHER_ORDERS = ((0, 1, 2), (2, 0, 1))
SCATTER_ORDERS = ((2, 1, 0), (1, 0, 2))
CHUNK = 256


def factor(count):
    return {16: (4, 2, 2), 64: (4, 4, 4)}.get(count, (count, 1, 1))


class Place:
    def __init__(self, dims):
        self.dims = dims
        mine = lax.axis_index("dp")
        n0, n1, n2 = dims
        self.at = (lax.rem(mine // (n1 * n2), n0), lax.rem(mine // n2, n1), lax.rem(mine, n2))

    def peer(self, dim, step):
        return lax.rem(self.at[dim] + step, self.dims[dim])

    def device(self, dim, coord):
        digits = list(self.at)
        digits[dim] = coord
        return {"dp": (digits[0] * self.dims[1] + digits[1]) * self.dims[2] + digits[2]}


def view(ref, fixed, columns):
    picks = tuple(fixed.get(d, slice(None)) for d in range(3))
    return ref.at[picks + (slice(None), pl.ds(columns[0], columns[1]))]


def entry_barrier(place):
    barrier = pltpu.get_barrier_semaphore()
    total = 0
    for dim in range(3):
        for step in range(1, place.dims[dim]):
            pl.semaphore_signal(
                barrier,
                inc=1,
                device_id=place.device(dim, place.peer(dim, step)),
                device_id_type=MESH_ID,
            )
            total += 1
    pl.semaphore_wait(barrier, total)


class GatherChunk:
    def __init__(self, place, shard, full, columns, order, send, recv, local):
        self.place, self.shard, self.full, self.columns = place, shard, full, columns
        self.order, self.send, self.recv, self.local = order, send, recv, local

    def copies(self, stage, arriving):
        place, dim, made = self.place, self.order[stage], []
        for step in range(1, place.dims[dim]):
            fixed = {d: place.at[d] for d in self.order[stage:]}
            if arriving:
                fixed[dim] = place.peer(dim, place.dims[dim] - step)
            target = view(self.full, fixed, self.columns)
            source = target
            if stage == 0 and not arriving:
                source = self.shard.at[:, pl.ds(*self.columns)]
            made.append(
                pltpu.make_async_remote_copy(
                    src_ref=source,
                    dst_ref=target,
                    send_sem=self.send.at[stage, step - 1],
                    recv_sem=self.recv.at[stage, step - 1],
                    device_id=place.device(dim, place.peer(dim, step)),
                    device_id_type=MESH_ID,
                )
            )
        return made

    def own(self):
        fixed = {d: self.place.at[d] for d in range(3)}
        return pltpu.make_async_copy(
            self.shard.at[:, pl.ds(*self.columns)],
            view(self.full, fixed, self.columns),
            self.local,
        )

    def act(self, phase):
        if phase == 0:
            self.own().start()
        else:
            if phase == 1:
                self.own().wait()
            for copy in self.copies(phase - 1, True):
                copy.wait_recv()
        if phase < 3:
            for copy in self.copies(phase, False):
                copy.start()
        else:
            for stage in range(3):
                for copy in self.copies(stage, False):
                    copy.wait_send()


class ScatterChunk:
    def __init__(self, place, grad, out, columns, order, buffers, send, recv, local):
        self.place, self.grad, self.out, self.columns = place, grad, out, columns
        self.order, self.send, self.recv, self.local = order, send, recv, local
        self.total, self.landings = buffers[0], buffers[1:]
        self.rest = [d for d in range(3) if d != order[0]]

    def pick(self, second, third):
        return tuple(second if d == self.order[1] else third for d in self.rest)

    def copies(self, stage, arriving):
        place, dim, made = self.place, self.order[stage], []
        for step in range(1, place.dims[dim]):
            to = place.peer(dim, step)
            land = self.landings[stage].at[step - 1]
            if arriving:
                source = land
            elif stage == 0:
                source = view(self.grad, {dim: to}, self.columns)
            elif stage == 1:
                source = self.total.at[self.pick(to, slice(None))]
            else:
                source = self.total.at[self.pick(place.at[self.order[1]], to)]
            made.append(
                pltpu.make_async_remote_copy(
                    src_ref=source,
                    dst_ref=land,
                    send_sem=self.send.at[stage, step - 1],
                    recv_sem=self.recv.at[stage, step - 1],
                    device_id=place.device(dim, to),
                    device_id_type=MESH_ID,
                )
            )
        return made

    def own(self):
        first = self.order[0]
        return pltpu.make_async_copy(
            view(self.grad, {first: self.place.at[first]}, self.columns), self.total, self.local
        )

    def act(self, phase):
        place, order = self.place, self.order
        if phase == 0:
            self.own().start()
        else:
            for copy in self.copies(phase - 1, True):
                copy.wait_recv()
        if phase == 1:
            self.own().wait()
            outer, inner = (place.dims[d] for d in self.rest)

            def add_first(item, carry):
                i, j = item // inner, lax.rem(item, inner)
                value = self.total[i, j].astype(F32)
                for slot in range(place.dims[order[0]] - 1):
                    value = value + self.landings[0][slot, i, j].astype(F32)
                self.total[i, j] = value.astype(BF16)
                return carry

            lax.fori_loop(0, outer * inner, add_first, 0)
        if phase == 2:

            def add_second(item, carry):
                spot = self.pick(place.at[order[1]], item)
                value = self.total[spot].astype(F32)
                for slot in range(place.dims[order[1]] - 1):
                    value = value + self.landings[1][slot, item].astype(F32)
                self.total[spot] = value.astype(BF16)
                return carry

            lax.fori_loop(0, place.dims[order[2]], add_second, 0)
        if phase < 3:
            for copy in self.copies(phase, False):
                copy.start()
        else:
            value = self.total[self.pick(place.at[order[1]], place.at[order[2]])].astype(F32)
            for slot in range(place.dims[order[2]] - 1):
                value = value + self.landings[2][slot].astype(F32)
            self.out[:, self.columns[0] : self.columns[0] + self.columns[1]] = value
            for stage in range(3):
                for copy in self.copies(stage, False):
                    copy.wait_send()


def chunks_of(widths):
    first, second = [], []
    for which, width in enumerate(widths):
        count = width // CHUNK
        later = max(1, round(count * 4 / 11))
        for i in range(count):
            (first if i < count - later else second).append((which, (i * CHUNK, CHUNK)))
    return first, second


def slots_of(first, second, stride=2):
    rows = []
    for slot in range(max(first, second) + 3 * stride):
        row = []
        for phase in (3, 2, 1, 0):
            if 0 <= slot - phase * stride < first:
                row.append((0, slot - phase * stride, phase))
            for chunk in range(second):
                if round(chunk * max(1, first) / max(1, second)) + phase * stride == slot:
                    row.append((1, chunk, phase))
        rows.append(row)
    return rows


class Gather:
    def __init__(self, shards, dims):
        self.dims, self.operands = dims, list(shards)
        self.widths = [shard.shape[1] for shard in shards]
        self.rows = shards[0].shape[0]
        self.plan = chunks_of(self.widths)
        self.count = sum(len(p) for p in self.plan)
        self.slots = slots_of(*(len(p) for p in self.plan))
        self.in_specs = [ANYWHERE] * len(shards)
        self.out_specs = [ANYWHERE] * len(shards)
        self.out_shape = [
            jax.ShapeDtypeStruct(dims + (self.rows, width), BF16) for width in self.widths
        ]
        most = max(dims) - 1
        self.scratch = [
            pltpu.SemaphoreType.DMA((self.count, 3, max(1, most))),
            pltpu.SemaphoreType.DMA((self.count, 3, max(1, most))),
            pltpu.SemaphoreType.DMA((self.count,)),
        ]

    def chunks(self, place, ins, outs, scratch):
        send, recv, local = scratch
        made, number = [], 0
        for order, plan in zip(GATHER_ORDERS, self.plan):
            group = []
            for which, columns in plan:
                group.append(
                    GatherChunk(
                        place,
                        ins[which],
                        outs[which],
                        columns,
                        order,
                        send.at[number],
                        recv.at[number],
                        local.at[number],
                    )
                )
                number += 1
            made.append(group)
        return made


class Scatter:
    def __init__(self, grads, dims):
        self.dims = dims
        total = dims[0] * dims[1] * dims[2]
        self.rows = grads[0].shape[0] // total
        self.widths = [grad.shape[1] for grad in grads]
        self.operands = [grad.reshape(dims + (self.rows, grad.shape[1])) for grad in grads]
        self.plan = chunks_of(self.widths)
        self.count = sum(len(p) for p in self.plan)
        self.slots = slots_of(*(len(p) for p in self.plan))
        self.in_specs = [ANYWHERE] * len(grads)
        self.out_specs = [pl.BlockSpec(memory_space=pltpu.VMEM)] * len(grads)
        self.out_shape = [jax.ShapeDtypeStruct((self.rows, width), F32) for width in self.widths]
        self.scratch = []
        for order, plan in zip(SCATTER_ORDERS, self.plan):
            c, b, a = order
            rest = tuple(dims[d] for d in range(3) if d != c)
            tile = (self.rows, CHUNK)
            held = max(1, len(plan))
            for lead in (
                rest,
                (max(1, dims[c] - 1),) + rest,
                (max(1, dims[b] - 1), dims[a]),
                (max(1, dims[a] - 1),),
            ):
                self.scratch.append(pltpu.VMEM((held,) + lead + tile, BF16))
        most = max(1, max(dims) - 1)
        self.scratch += [
            pltpu.SemaphoreType.DMA((self.count, 3, most)),
            pltpu.SemaphoreType.DMA((self.count, 3, most)),
            pltpu.SemaphoreType.DMA((self.count,)),
        ]

    def chunks(self, place, ins, outs, scratch):
        send, recv, local = scratch[8:]
        made, number = [], 0
        for side, (order, plan) in enumerate(zip(SCATTER_ORDERS, self.plan)):
            group = []
            for at, (which, columns) in enumerate(plan):
                group.append(
                    ScatterChunk(
                        place,
                        ins[which],
                        outs[which],
                        columns,
                        order,
                        [buffer.at[at] for buffer in scratch[4 * side : 4 * side + 4]],
                        send.at[number],
                        recv.at[number],
                        local.at[number],
                    )
                )
                number += 1
            made.append(group)
        return made


def transfer(plan, collective_id):
    def kernel(*refs):
        ins = refs[: len(plan.in_specs)]
        outs = refs[len(ins) : len(ins) + len(plan.out_specs)]
        place = Place(plan.dims)
        entry_barrier(place)
        groups = plan.chunks(place, ins, outs, refs[len(ins) + len(outs) :])
        for row in plan.slots:
            for order, chunk, phase in row:
                groups[order][chunk].act(phase)

    return pl.pallas_call(
        kernel,
        out_shape=plan.out_shape,
        in_specs=plan.in_specs,
        out_specs=plan.out_specs,
        scratch_shapes=plan.scratch,
        compiler_params=pltpu.CompilerParams(
            collective_id=collective_id, has_side_effects=True, vmem_limit_bytes=VMEM_BYTES
        ),
    )(*plan.operands)


def share_all(message, collective_id):
    dp, tensor = lax.axis_size("dp"), lax.axis_size("tensor")
    total = dp * tensor
    rows = message.shape[0]

    def kernel(message_ref, out_ref, held, send, recv):
        mine = lax.axis_index("dp") * tensor + lax.axis_index("tensor")

        def at(step):
            number = lax.rem(mine + step, total)
            return {"dp": number // tensor, "tensor": lax.rem(number, tensor)}

        barrier = pltpu.get_barrier_semaphore()

        def greet(step, carry):
            pl.semaphore_signal(barrier, inc=1, device_id=at(step), device_id_type=MESH_ID)
            return carry

        lax.fori_loop(1, total, greet, 0)
        pl.semaphore_wait(barrier, total - 1)

        def copy(step, slot):
            return pltpu.make_async_remote_copy(
                src_ref=message_ref,
                dst_ref=held.at[slot],
                send_sem=send.at[step],
                recv_sem=recv.at[step],
                device_id=at(step),
                device_id_type=MESH_ID,
            )

        def start(step, carry):
            copy(step, mine).start()
            return carry

        lax.fori_loop(1, total, start, 0)
        held[mine] = message_ref[...]

        def finish(step, carry):
            copy(step, lax.rem(mine + total - step, total)).wait_recv()
            return carry

        lax.fori_loop(1, total, finish, 0)

        def sent(step, carry):
            copy(step, mine).wait_send()
            return carry

        lax.fori_loop(1, total, sent, 0)
        out_ref[...] = held[...]

    out = pl.pallas_call(
        kernel,
        out_shape=jax.ShapeDtypeStruct((total, rows, 128), F32),
        in_specs=[pl.BlockSpec(memory_space=pltpu.VMEM)],
        out_specs=pl.BlockSpec(memory_space=pltpu.VMEM),
        scratch_shapes=[
            pltpu.VMEM((total, rows, 128), F32),
            pltpu.SemaphoreType.DMA((total,)),
            pltpu.SemaphoreType.DMA((total,)),
        ],
        compiler_params=pltpu.CompilerParams(collective_id=collective_id, has_side_effects=True),
    )(message)
    return out.reshape(dp, tensor, rows, 128)


def rotary_tables():
    half_size = HEAD_WIDTH // 2
    frequency = jnp.power(
        theta_base, -2.0 * jnp.arange(half_size, dtype=F32) / HEAD_WIDTH
    )
    angles = frequency[:, None] * jnp.arange(SEQUENCE_LENGTH, dtype=F32)[None, :]
    return jnp.cos(angles), jnp.sin(angles)


def rotate(values, cosine, sine, sign):
    half = HEAD_WIDTH // 2
    top, bottom = values[:half], values[half:]
    return jnp.concatenate(
        [top * cosine - sign * (bottom * sine), bottom * cosine + sign * (top * sine)], 0
    )


def product(left, right, left_dim=1, right_dim=0):
    return lax.dot_general(
        left, right, (((left_dim,), (right_dim,)), ((), ())), preferred_element_type=F32
    )


def row_scale(values):
    return lax.rsqrt(jnp.mean(values * values, -1, keepdims=True) + norm_eps)


def compute_call(kernel, name, **kwargs):
    return pl.pallas_call(
        kernel,
        name=name,
        compiler_params=pltpu.CompilerParams(vmem_limit_bytes=VMEM_BYTES),
        **kwargs,
    )


def project(rows, gain, weights, cosine, sine):
    tokens, width = rows.shape
    features = weights.shape[1]
    block = 512
    turned = features * 3 // 4

    def kernel(x_ref, gain_ref, w_ref, cos_ref, sin_ref, n_ref, out_ref):
        x = x_ref[...].astype(F32)
        normed = (x * row_scale(x) * gain_ref[...]).astype(BF16)
        n_ref[...] = normed
        raw = product(w_ref[...], normed, 0, 1)
        cosine, sine = cos_ref[...], sin_ref[...]
        for first in range(0, turned, HEAD_WIDTH):
            rows = slice(first, first + HEAD_WIDTH)
            out_ref[rows] = rotate(raw[rows], cosine, sine, 1.0).astype(BF16)
        out_ref[turned:] = raw[turned:].astype(BF16)

    per_sequence = SEQUENCE_LENGTH // block
    table = pl.BlockSpec((HEAD_WIDTH // 2, block), lambda i: (0, lax.rem(i, per_sequence)))
    return compute_call(
        kernel,
        "project",
        grid=(tokens // block,),
        in_specs=[
            pl.BlockSpec((block, width), lambda i: (i, 0)),
            pl.BlockSpec((1, width), lambda i: (0, 0)),
            pl.BlockSpec((width, features), lambda i: (0, 0)),
            table,
            table,
        ],
        out_specs=[
            pl.BlockSpec((block, width), lambda i: (i, 0)),
            pl.BlockSpec((features, block), lambda i: (0, i)),
        ],
        out_shape=[
            jax.ShapeDtypeStruct((tokens, width), BF16),
            jax.ShapeDtypeStruct((features, tokens), BF16),
        ],
    )(rows, gain, weights, cosine, sine)


def visible(prefix, first):
    place = lax.broadcasted_iota(jnp.int32, (1, QUERY_CHUNK), 1) + first
    limit = jnp.maximum(place + 1, prefix)
    return lax.broadcasted_iota(jnp.int32, (SEQUENCE_LENGTH, QUERY_CHUNK), 0) < limit


def attention_specs(features):
    kv_heads = features // HEAD_WIDTH // (GROUP_WIDTH + 2)
    q_heads = kv_heads * GROUP_WIDTH
    wide = (GROUP_WIDTH * HEAD_WIDTH, SEQUENCE_LENGTH)
    slim = (HEAD_WIDTH, SEQUENCE_LENGTH)
    query = pl.BlockSpec(wide, lambda s, j, p: (j, s))
    key = pl.BlockSpec(slim, lambda s, j, p: (q_heads + j, s))
    value = pl.BlockSpec(slim, lambda s, j, p: (q_heads + kv_heads + j, s))
    sums = pl.BlockSpec((None, GROUP_WIDTH, SEQUENCE_LENGTH), lambda s, j, p: (j, 0, s))
    return kv_heads, q_heads, query, key, value, sums


def attend_forward(qkv, prefixes):
    features, tokens = qkv.shape
    kv_heads, q_heads, query, key, value, sums = attention_specs(features)
    scale = SCORE_SCALE * LOG2_E

    def kernel(prefix_ref, q_ref, k_ref, v_ref, mixed_ref, sum_ref):
        prefix = prefix_ref[pl.program_id(0)]
        keys = k_ref[...].T
        values = jnp.concatenate([v_ref[...], jnp.ones((16, SEQUENCE_LENGTH), BF16)], 0)
        for head in range(GROUP_WIDTH):
            rows = slice(head * HEAD_WIDTH, (head + 1) * HEAD_WIDTH)
            for first in range(0, SEQUENCE_LENGTH, QUERY_CHUNK):
                columns = slice(first, first + QUERY_CHUNK)
                scores = product(keys, q_ref[rows, columns])
                scores = jnp.where(visible(prefix, first), scores, neg_fill)
                peak = jnp.max(scores, 0, keepdims=True) * scale
                weights = jnp.exp2(scores * scale - peak).astype(BF16)
                out = product(values, weights)
                total = out[HEAD_WIDTH : HEAD_WIDTH + 1]
                mixed_ref[rows, columns] = (out[:HEAD_WIDTH] * (1.0 / total)).astype(BF16)
                sum_ref[head : head + 1, columns] = peak + jnp.log2(total)

    return compute_call(
        kernel,
        "attend_forward",
        grid_spec=pltpu.PrefetchScalarGridSpec(
            num_scalar_prefetch=1,
            grid=(tokens // SEQUENCE_LENGTH, kv_heads),
            in_specs=[query, key, value],
            out_specs=[query, sums],
        ),
        out_shape=[
            jax.ShapeDtypeStruct((q_heads * HEAD_WIDTH, tokens), BF16),
            jax.ShapeDtypeStruct((kv_heads, GROUP_WIDTH, tokens), F32),
        ],
    )(prefixes, qkv, qkv, qkv)


def attend_backward(qkv, dmixed, mixed, logsums, prefixes, cosine, sine):
    features, tokens = qkv.shape
    kv_heads, q_heads, query, key, value, sums = attention_specs(features)
    scale = SCORE_SCALE * LOG2_E

    def kernel(
        prefix_ref,
        q_ref,
        k_ref,
        v_ref,
        d_ref,
        mixed_ref,
        sum_ref,
        cos_ref,
        sin_ref,
        dq_ref,
        dk_ref,
        dv_ref,
    ):
        prefix = prefix_ref[pl.program_id(0)]
        keys_flat = k_ref[...]
        keys, values = keys_flat.T, v_ref[...].T
        dkeys = jnp.zeros((SEQUENCE_LENGTH, HEAD_WIDTH), F32)
        dvalues = jnp.zeros((SEQUENCE_LENGTH, HEAD_WIDTH), F32)
        cosine, sine = cos_ref[...], sin_ref[...]
        for head in range(GROUP_WIDTH):
            rows = slice(head * HEAD_WIDTH, (head + 1) * HEAD_WIDTH)
            for first in range(0, SEQUENCE_LENGTH, QUERY_CHUNK):
                columns = slice(first, first + QUERY_CHUNK)
                q, d = q_ref[rows, columns], d_ref[rows, columns]
                delta = jnp.sum(
                    d.astype(F32) * mixed_ref[rows, columns].astype(F32), 0, keepdims=True
                )
                scores = product(keys, q) * scale
                weights = jnp.exp2(scores - sum_ref[head : head + 1, columns])
                weights = jnp.where(visible(prefix, first), weights, 0.0)
                dweights = product(values, d)
                dscores = (weights * (dweights - delta)).astype(BF16)
                dvalues = dvalues + product(weights.astype(BF16), d.T)
                dkeys = dkeys + product(dscores, q.T)
                dq = product(keys_flat, dscores) * SCORE_SCALE
                dq_ref[rows, columns] = rotate(
                    dq, cosine[:, columns], sine[:, columns], -1.0
                ).astype(BF16)
        dk_ref[...] = rotate((dkeys * SCORE_SCALE).T, cosine, sine, -1.0).astype(BF16)
        dv_ref[...] = dvalues.T.astype(BF16)

    slim = pl.BlockSpec((HEAD_WIDTH, SEQUENCE_LENGTH), lambda s, j, p: (j, s))
    table = pl.BlockSpec((HEAD_WIDTH // 2, SEQUENCE_LENGTH), lambda s, j, p: (0, 0))
    return compute_call(
        kernel,
        "attend_backward",
        grid_spec=pltpu.PrefetchScalarGridSpec(
            num_scalar_prefetch=1,
            grid=(tokens // SEQUENCE_LENGTH, kv_heads),
            in_specs=[query, key, value, query, query, sums, table, table],
            out_specs=[query, slim, slim],
        ),
        out_shape=[
            jax.ShapeDtypeStruct((q_heads * HEAD_WIDTH, tokens), BF16),
            jax.ShapeDtypeStruct((kv_heads * HEAD_WIDTH, tokens), BF16),
            jax.ShapeDtypeStruct((kv_heads * HEAD_WIDTH, tokens), BF16),
        ],
    )(prefixes, qkv, qkv, qkv, dmixed, mixed, logsums, cosine, sine)


def feed_forward(rows, gate_full, up_full):
    tokens, width = rows.shape
    units = gate_full.shape[1]
    tall, wide = 1024, 512

    def kernel(n_ref, gate_w, up_w, gate_ref, up_ref, hidden_ref):
        normed = n_ref[...]
        gate = product(normed, gate_w[...])
        up = product(normed, up_w[...])
        gate_ref[...] = gate.astype(BF16)
        up_ref[...] = up.astype(BF16)
        hidden_ref[...] = (gate * jax.nn.sigmoid(gate) * up).astype(BF16)

    weight = pl.BlockSpec((width, wide), lambda i, j: (0, j))
    out = pl.BlockSpec((tall, wide), lambda i, j: (i, j))
    return compute_call(
        kernel,
        "feed_forward",
        grid=(tokens // tall, units // wide),
        in_specs=[pl.BlockSpec((tall, width), lambda i, j: (i, 0)), weight, weight],
        out_specs=[out, out, out],
        out_shape=[jax.ShapeDtypeStruct((tokens, units), BF16)] * 3,
    )(rows, gate_full, up_full)


def feed_backward(back_rows, down_full, gate, up):
    tokens, width = back_rows.shape
    units = down_full.shape[1]
    tall, wide = 1024, 512

    def kernel(d_ref, down_w, gate_ref, up_ref, dgate_ref, dup_ref):
        dhidden = product(d_ref[...], down_w[...])
        gate = gate_ref[...].astype(F32)
        sigmoid = jax.nn.sigmoid(gate)
        dup_ref[...] = (dhidden * gate * sigmoid).astype(BF16)
        dgate_ref[...] = (
            dhidden * up_ref[...].astype(F32) * sigmoid * (1.0 + gate * (1.0 - sigmoid))
        ).astype(BF16)

    tile = pl.BlockSpec((tall, wide), lambda i, j: (i, j))
    return compute_call(
        kernel,
        "feed_backward",
        grid=(tokens // tall, units // wide),
        in_specs=[
            pl.BlockSpec((tall, width), lambda i, j: (i, 0)),
            pl.BlockSpec((width, wide), lambda i, j: (0, j)),
            tile,
            tile,
        ],
        out_specs=[tile, tile],
        out_shape=[jax.ShapeDtypeStruct((tokens, units), BF16)] * 2,
    )(back_rows, down_full, gate, up)


def second_norm_grad(dgate, dup, gate_full, up_full):
    tokens, units = dgate.shape
    width = gate_full.shape[0]
    block = 256

    def kernel(dgate_ref, dup_ref, gate_w, up_w, out_ref):
        out_ref[...] = (
            product(dgate_ref[...], gate_w[...], 1, 1) + product(dup_ref[...], up_w[...], 1, 1)
        ).astype(BF16)

    rows = pl.BlockSpec((block, units), lambda i: (i, 0))
    weight = pl.BlockSpec((width, units), lambda i: (0, 0), pipeline_mode=pl.Buffered(1))
    return compute_call(
        kernel,
        "second_norm_grad",
        grid=(tokens // block,),
        in_specs=[rows, rows, weight, weight],
        out_specs=pl.BlockSpec((block, width), lambda i: (i, 0)),
        out_shape=jax.ShapeDtypeStruct((tokens, width), BF16),
    )(dgate, dup, gate_full, up_full)


def tensor_sum(partial):
    other = lax.ppermute(partial, "tensor", [(0, 1), (1, 0)])
    return partial.astype(F32) + other.astype(F32)


def norm_back(dnorm, gain_row, unit_rows, inverse):
    scaled = dnorm * gain_row
    return inverse * (scaled - unit_rows * jnp.mean(scaled * unit_rows, -1, keepdims=True))


def adam_step(weight, gradient, first_moment, second_moment, rate, decay, factor, fix_one, fix_two):
    clipped = factor * gradient
    first_new = beta_one * first_moment + (1.0 - beta_one) * clipped
    second_new = beta_two * second_moment + (1.0 - beta_two) * clipped * clipped
    update = first_new / fix_one / (jnp.sqrt(second_new / fix_two) + adam_eps) + decay * weight
    return (weight - rate * update, first_new, second_new)


def local(
    block_in,
    prefix_len,
    out_grad,
    step_count,
    q_weight,
    key_matrix,
    value_matrix,
    o_weight,
    gate_weight,
    up_weight,
    down_weight,
    norm_gains,
    query_mean_moment,
    key_mean_moment,
    value_mean_moment,
    output_mean_moment,
    gate_mean_moment,
    up_mean_moment,
    down_mean_moment,
    gains_mean_moment,
    q_second,
    key_square_moment,
    value_square_moment,
    o_second,
    gate_second,
    up_second,
    down_second,
    gains_second,
):
    dims = factor(lax.axis_size("dp"))
    width = block_in.shape[1]
    q_width, kv_width = q_weight.shape[1], key_matrix.shape[1]
    units = gate_weight.shape[1]
    qkv_low = jnp.concatenate([q_weight, key_matrix, value_matrix], 1).astype(BF16)
    (qkv_full,) = transfer(Gather([qkv_low], dims), 0)
    o_full, gate_full, up_full, down_full = transfer(
        Gather([w.astype(BF16) for w in (o_weight, gate_weight, up_weight, down_weight)], dims), 1
    )
    qkv_full = qkv_full.reshape(width, -1)
    o_full = o_full.reshape(width, -1)
    gate_full, up_full, down_full = (
        w.reshape(width, units) for w in (gate_full, up_full, down_full)
    )
    cosine, sine = rotary_tables()

    normed_one, qkv = project(block_in, norm_gains[:1], qkv_full, cosine, sine)
    mixed, logsums = attend_forward(qkv, prefix_len)
    input_rows = block_in.astype(F32)
    middle = input_rows + tensor_sum(product(mixed, o_full, 0, 1).astype(BF16))
    inverse_two = row_scale(middle)
    normed_two = (middle * inverse_two * norm_gains[1]).astype(BF16)
    gate, up, hidden = feed_forward(normed_two, gate_full, up_full)

    grad_down = product(out_grad, hidden, 0, 0).astype(BF16)
    block_out = (middle + tensor_sum(product(hidden, down_full, 1, 1).astype(BF16))).astype(BF16)
    dgate, dup = feed_backward(out_grad, down_full, gate, up)
    grad_gate = product(normed_two, dgate, 0, 0).astype(BF16)
    grad_up = product(normed_two, dup, 0, 0).astype(BF16)
    dnorm_two = tensor_sum(second_norm_grad(dgate, dup, gate_full, up_full))
    unit_two = middle * inverse_two
    gain_two = jnp.sum(dnorm_two * unit_two, 0)
    dmiddle = out_grad.astype(F32) + norm_back(dnorm_two, norm_gains[1], unit_two, inverse_two)
    dmiddle_low = dmiddle.astype(BF16)
    grad_out = product(dmiddle_low, mixed, 0, 1).astype(BF16)
    dmixed = product(o_full, dmiddle_low, 0, 1).astype(BF16)
    dquery, dkey, dvalue = attend_backward(
        qkv, dmixed, mixed, logsums, prefix_len, cosine, sine
    )
    dqkv = jnp.concatenate([dquery, dkey, dvalue], 0)
    grad_qkv = product(normed_one, dqkv, 0, 1).astype(BF16)
    dnorm_one = tensor_sum(product(dqkv, qkv_full, 0, 1).astype(BF16))
    inverse_one = row_scale(input_rows)
    unit_one = input_rows * inverse_one
    gain_one = jnp.sum(dnorm_one * unit_one, 0)
    in_grad = dmiddle + norm_back(dnorm_one, norm_gains[0], unit_one, inverse_one)

    sum_qkv, sum_out, sum_gate, sum_up, sum_down = transfer(
        Scatter([grad_qkv, grad_out, grad_gate, grad_up, grad_down], dims), 2
    )
    shares = (sum_qkv, sum_out, sum_gate, sum_up, sum_down)
    squares = sum(jnp.sum(jnp.square(share)) for share in shares)
    gain_rows = 2 * width // 128
    message = jnp.concatenate(
        [
            jnp.stack([gain_one, gain_two]).reshape(gain_rows, 128),
            jnp.broadcast_to(squares, (8, 128)),
        ],
        0,
    )
    everyone = share_all(message, 3)
    gain_sum = jnp.sum(everyone[:, 0, :gain_rows], 0)
    total_square = jnp.sum(everyone[:, :, gain_rows, 0]) + jnp.sum(jnp.square(gain_sum))
    gain_width = width // lax.axis_size("dp")
    first_column = lax.axis_index("dp") * gain_width
    grad_gains = lax.dynamic_slice_in_dim(gain_sum.reshape(2, width), first_column, gain_width, 1)
    old_gains = lax.dynamic_slice_in_dim(norm_gains, first_column, gain_width, 1)
    reduced = (
        sum_qkv[:, :q_width],
        sum_qkv[:, q_width : q_width + kv_width],
        sum_qkv[:, q_width + kv_width :],
        sum_out,
        sum_gate,
        sum_up,
        sum_down,
        grad_gains,
    )
    grad_norm = jnp.sqrt(total_square)
    factor_now = jnp.minimum(1.0, clip_limit / grad_norm)
    step_float = step_count[0].astype(F32)
    fix_one = 1.0 - jnp.power(beta_one, step_float)
    fix_two = 1.0 - jnp.power(beta_two, step_float)
    masters = (
        q_weight,
        key_matrix,
        value_matrix,
        o_weight,
        gate_weight,
        up_weight,
        down_weight,
        old_gains,
    )
    firsts = (
        query_mean_moment,
        key_mean_moment,
        value_mean_moment,
        output_mean_moment,
        gate_mean_moment,
        up_mean_moment,
        down_mean_moment,
        gains_mean_moment,
    )
    seconds = (
        q_second,
        key_square_moment,
        value_square_moment,
        o_second,
        gate_second,
        up_second,
        down_second,
        gains_second,
    )
    rate_list = matrix_rates + (gain_rate,)
    decay_list = (decay_rate,) * 7 + (0.0,)
    new_weights, new_firsts, new_seconds = ([], [], [])
    for weight, gradient, first_moment, second_moment, rate, decay in zip(
        masters, reduced, firsts, seconds, rate_list, decay_list
    ):
        weight_new, first_new, second_new = adam_step(
            weight, gradient, first_moment, second_moment, rate, decay, factor_now, fix_one, fix_two
        )
        new_weights.append(weight_new)
        new_firsts.append(first_new)
        new_seconds.append(second_new)
    return (
        block_out,
        in_grad,
        grad_norm.reshape(1),
        new_weights[0],
        new_weights[1],
        new_weights[2],
        new_weights[3],
        new_weights[4],
        new_weights[5],
        new_weights[6],
        new_weights[7],
        new_firsts[0],
        new_firsts[1],
        new_firsts[2],
        new_firsts[3],
        new_firsts[4],
        new_firsts[5],
        new_firsts[6],
        new_firsts[7],
        new_seconds[0],
        new_seconds[1],
        new_seconds[2],
        new_seconds[3],
        new_seconds[4],
        new_seconds[5],
        new_seconds[6],
        new_seconds[7],
    )


def solution(mesh):
    return jax.shard_map(
        local,
        mesh=mesh,
        in_specs=(
            P("dp", None),
            P("dp"),
            P("dp", None),
            P(),
            P("dp", "tensor"),
            P("dp", "tensor"),
            P("dp", "tensor"),
            P("dp", "tensor"),
            P("dp", "tensor"),
            P("dp", "tensor"),
            P("dp", "tensor"),
            P(),
            P("dp", "tensor"),
            P("dp", "tensor"),
            P("dp", "tensor"),
            P("dp", "tensor"),
            P("dp", "tensor"),
            P("dp", "tensor"),
            P("dp", "tensor"),
            P(None, "dp"),
            P("dp", "tensor"),
            P("dp", "tensor"),
            P("dp", "tensor"),
            P("dp", "tensor"),
            P("dp", "tensor"),
            P("dp", "tensor"),
            P("dp", "tensor"),
            P(None, "dp"),
        ),
        out_specs=(
            P("dp", None),
            P("dp", None),
            P(),
            P("dp", "tensor"),
            P("dp", "tensor"),
            P("dp", "tensor"),
            P("dp", "tensor"),
            P("dp", "tensor"),
            P("dp", "tensor"),
            P("dp", "tensor"),
            P(None, "dp"),
            P("dp", "tensor"),
            P("dp", "tensor"),
            P("dp", "tensor"),
            P("dp", "tensor"),
            P("dp", "tensor"),
            P("dp", "tensor"),
            P("dp", "tensor"),
            P(None, "dp"),
            P("dp", "tensor"),
            P("dp", "tensor"),
            P("dp", "tensor"),
            P("dp", "tensor"),
            P("dp", "tensor"),
            P("dp", "tensor"),
            P("dp", "tensor"),
            P(None, "dp"),
        ),
        check_vma=False,
    )
```

```python
import enum
import math

import jax
import jax.numpy as jnp
from jax import lax
from jax.experimental import pallas as pl
from jax.experimental.pallas import tpu as pltpu
from jax.sharding import PartitionSpec as P

HEAD_WIDTH = 96
GROUP_WIDTH = 2
SEQUENCE_LENGTH = 1024
QUERY_CHUNK = 512
VMEM_BYTES = 62 * 2**20
LOG2_E = 1.4426950408889634
SCORE_SCALE = 1.0 / math.sqrt(HEAD_WIDTH)

theta_base = 100000.0
norm_eps = 1e-05
beta_one = 0.9
beta_two = 0.95
adam_eps = 1e-08
decay_rate = 0.1
clip_limit = 1.0
neg_fill = -1e30
matrix_rates = (0.08, 0.08, 0.08, 1.0, 0.08, 0.08, 0.1)
gain_rate = 1.0

BF16 = jnp.bfloat16
F32 = jnp.float32
ANYWHERE = pl.BlockSpec(memory_space=pl.ANY)
MESH_ID = pl.DeviceIdType.MESH
GATHER_ORDERS = ((0, 1, 2), (2, 0, 1))
SCATTER_ORDERS = ((2, 1, 0), (1, 0, 2))
CHUNK = 256
PARTIAL_COLUMNS = 512


class Name(enum.Enum):
    block_in = enum.auto()
    block_out = enum.auto()
    change = enum.auto()
    cosine = enum.auto()
    dgate = enum.auto()
    dmiddle = enum.auto()
    dmixed = enum.auto()
    down_full = enum.auto()
    dqkv = enum.auto()
    dup = enum.auto()
    gain_sum = enum.auto()
    gains = enum.auto()
    gate = enum.auto()
    gate_full = enum.auto()
    grad_down = enum.auto()
    grad_gate = enum.auto()
    grad_out = enum.auto()
    grad_qkv = enum.auto()
    grad_up = enum.auto()
    hidden = enum.auto()
    logsums = enum.auto()
    middle = enum.auto()
    mixed = enum.auto()
    normed_one = enum.auto()
    normed_two = enum.auto()
    o_full = enum.auto()
    out_grad = enum.auto()
    prefix = enum.auto()
    qkv = enum.auto()
    qkv_full = enum.auto()
    share_gain = enum.auto()
    share_square = enum.auto()
    sine = enum.auto()
    square_sum = enum.auto()
    squares = enum.auto()
    sum_down = enum.auto()
    sum_gate = enum.auto()
    sum_out = enum.auto()
    sum_qkv = enum.auto()
    sum_up = enum.auto()
    swap = enum.auto()
    up = enum.auto()
    up_full = enum.auto()


def factor(count):
    return {16: (4, 2, 2), 64: (4, 4, 4)}.get(count, (count, 1, 1))


class Place:
    def __init__(self, dims):
        self.dims = dims
        mine = lax.axis_index("dp")
        n0, n1, n2 = dims
        self.at = (lax.rem(mine // (n1 * n2), n0), lax.rem(mine // n2, n1), lax.rem(mine, n2))

    def peer(self, dim, step):
        return lax.rem(self.at[dim] + step, self.dims[dim])

    def device(self, dim, coord):
        digits = list(self.at)
        digits[dim] = coord
        return {"dp": (digits[0] * self.dims[1] + digits[1]) * self.dims[2] + digits[2]}


def view(ref, fixed, columns):
    picks = tuple(fixed.get(d, slice(None)) for d in range(3))
    return ref.at[picks + (slice(None), pl.ds(columns[0], columns[1]))]


def entry_barrier(place):
    barrier = pltpu.get_barrier_semaphore()
    total = 0
    for dim in range(3):
        for step in range(1, place.dims[dim]):
            pl.semaphore_signal(
                barrier,
                inc=1,
                device_id=place.device(dim, place.peer(dim, step)),
                device_id_type=MESH_ID,
            )
            total += 1
    pl.semaphore_signal(
        barrier, inc=1, device_id={"tensor": 1 - lax.axis_index("tensor")}, device_id_type=MESH_ID
    )
    pl.semaphore_wait(barrier, total + 1)


class Exchange:
    def __init__(self, refs):
        self.own, self.other, self.send, self.recv, self.free = (
            refs[Name.swap, part] for part in range(5)
        )
        self.peer = {"tensor": 1 - lax.axis_index("tensor")}

    def copy(self, number, rows, columns):
        return pltpu.make_async_remote_copy(
            src_ref=self.own.at[rows, columns],
            dst_ref=self.other.at[rows, columns],
            send_sem=self.send.at[number],
            recv_sem=self.recv.at[number],
            device_id=self.peer,
            device_id_type=MESH_ID,
        )

    @staticmethod
    def release(refs):
        here = Exchange(refs)
        pl.semaphore_signal(here.free, inc=1, device_id=here.peer, device_id_type=MESH_ID)

    @staticmethod
    def claim(refs):
        pl.semaphore_wait(refs[Name.swap, 4], 1)

    @staticmethod
    def scratch(tokens, width, count):
        kinds = (
            pltpu.VMEM((tokens, width), BF16),
            pltpu.VMEM((tokens, width), BF16),
            pltpu.SemaphoreType.DMA((count,)),
            pltpu.SemaphoreType.DMA((count,)),
            pltpu.SemaphoreType.REGULAR,
        )
        return {(Name.swap, part): kind for part, kind in enumerate(kinds)}


class GatherChunk:
    def __init__(self, place, master, shard, full, columns, order, send, recv, local):
        self.place, self.shard, self.full, self.columns = place, shard, full, columns
        self.order, self.send, self.recv, self.local = order, send, recv, local
        self.master = master

    def copies(self, stage, arriving):
        place, dim, made = self.place, self.order[stage], []
        for step in range(1, place.dims[dim]):
            fixed = {d: place.at[d] for d in self.order[stage:]}
            if arriving:
                fixed[dim] = place.peer(dim, place.dims[dim] - step)
            target = view(self.full, fixed, self.columns)
            source = target
            if stage == 0 and not arriving:
                source = self.shard.at[:, pl.ds(*self.columns)]
            made.append(
                pltpu.make_async_remote_copy(
                    src_ref=source,
                    dst_ref=target,
                    send_sem=self.send.at[stage, step - 1],
                    recv_sem=self.recv.at[stage, step - 1],
                    device_id=place.device(dim, place.peer(dim, step)),
                    device_id_type=MESH_ID,
                )
            )
        return made

    def own(self):
        fixed = {d: self.place.at[d] for d in range(3)}
        return pltpu.make_async_copy(
            self.shard.at[:, pl.ds(*self.columns)],
            view(self.full, fixed, self.columns),
            self.local,
        )

    def act(self, phase):
        if phase == 0:
            columns = slice(self.columns[0], self.columns[0] + self.columns[1])
            self.shard[:, columns] = self.master[:, columns].astype(BF16)
            self.own().start()
        else:
            if phase == 1:
                self.own().wait()
            for copy in self.copies(phase - 1, True):
                copy.wait_recv()
        if phase < 3:
            for copy in self.copies(phase, False):
                copy.start()
        else:
            for stage in range(3):
                for copy in self.copies(stage, False):
                    copy.wait_send()


class ScatterChunk:
    def __init__(
        self, place, grad, out, squares, columns, order, mine, landings, send, recv, local
    ):
        self.place, self.grad, self.out, self.columns = place, grad, out, columns
        self.order, self.send, self.recv, self.local = order, send, recv, local
        self.squares, self.mine, self.landings = squares, mine, landings
        self.total = landings[0].at[0]
        self.rest = [d for d in range(3) if d != order[0]]

    def pick(self, second, third):
        return tuple(second if d == self.order[1] else third for d in self.rest)

    def copies(self, stage, arriving):
        place, dim, made = self.place, self.order[stage], []
        for step in range(1, place.dims[dim]):
            to = place.peer(dim, step)
            land = self.landings[stage].at[step - 1]
            if arriving:
                source = land
            elif stage == 0:
                source = view(self.grad, {dim: to}, self.columns)
            elif stage == 1:
                source = self.total.at[self.pick(to, slice(None))]
            else:
                source = self.total.at[self.pick(place.at[self.order[1]], to)]
            made.append(
                pltpu.make_async_remote_copy(
                    src_ref=source,
                    dst_ref=land,
                    send_sem=self.send.at[stage, step - 1],
                    recv_sem=self.recv.at[stage, step - 1],
                    device_id=place.device(dim, to),
                    device_id_type=MESH_ID,
                )
            )
        return made

    def own(self):
        first = self.order[0]
        return pltpu.make_async_copy(
            view(self.grad, {first: self.place.at[first]}, self.columns), self.mine, self.local
        )

    def act(self, phase):
        place, order = self.place, self.order
        if phase == 0:
            self.own().start()
        else:
            for copy in self.copies(phase - 1, True):
                copy.wait_recv()
        if phase == 1:
            self.own().wait()
            outer, inner = (place.dims[d] for d in self.rest)

            def add_first(item, carry):
                i, j = item // inner, lax.rem(item, inner)
                value = self.mine[i, j].astype(F32)
                for slot in range(place.dims[order[0]] - 1):
                    value = value + self.landings[0][slot, i, j].astype(F32)
                self.total[i, j] = value.astype(BF16)
                return carry

            lax.fori_loop(0, outer * inner, add_first, 0)
        if phase == 2:

            def add_second(item, carry):
                spot = self.pick(place.at[order[1]], item)
                value = self.total[spot].astype(F32)
                for slot in range(place.dims[order[1]] - 1):
                    value = value + self.landings[1][slot, item].astype(F32)
                self.total[spot] = value.astype(BF16)
                return carry

            lax.fori_loop(0, place.dims[order[2]], add_second, 0)
        if phase < 3:
            for copy in self.copies(phase, False):
                copy.start()
        else:
            value = self.total[self.pick(place.at[order[1]], place.at[order[2]])].astype(F32)
            for slot in range(place.dims[order[2]] - 1):
                value = value + self.landings[2][slot].astype(F32)
            self.out[:, self.columns[0] : self.columns[0] + self.columns[1]] = value
            self.squares[...] += jnp.sum(value * value, 0, keepdims=True)
            for stage in range(3):
                for copy in self.copies(stage, False):
                    copy.wait_send()


def chunks_of(widths):
    first, second = [], []
    for which, width in enumerate(widths):
        count = width // CHUNK
        later = max(1, round(count * 4 / 11))
        for i in range(count):
            (first if i < count - later else second).append((which, (i * CHUNK, CHUNK)))
    return first, second


def slots_of(first, second, stride=2):
    rows = []
    for slot in range(max(first, second) + 3 * stride):
        row = []
        for phase in (3, 2, 1, 0):
            if 0 <= slot - phase * stride < first:
                row.append((0, slot - phase * stride, phase))
            for chunk in range(second):
                if round(chunk * max(1, first) / max(1, second)) + phase * stride == slot:
                    row.append((1, chunk, phase))
        rows.append(row)
    return rows


class Gather:
    def __init__(self, shards, dims):
        self.dims, self.names = dims, list(shards)
        self.parts = [[part.shape[1] for part in parts] for parts in shards.values()]
        self.operands = [part for parts in shards.values() for part in parts]
        self.widths = [sum(widths) for widths in self.parts]
        self.rows = self.operands[0].shape[0]
        self.plan = chunks_of(self.widths)
        self.count = sum(len(p) for p in self.plan)
        self.slots = slots_of(*(len(p) for p in self.plan))
        self.in_specs = [ANYWHERE] * len(self.operands)
        self.out_specs = [ANYWHERE] * len(shards)
        self.out_shape = [
            jax.ShapeDtypeStruct(dims + (self.rows, width), BF16) for width in self.widths
        ]
        most = max(1, max(dims) - 1)
        self.scratch = [
            pltpu.SemaphoreType.DMA((self.count, 3, most)),
            pltpu.SemaphoreType.DMA((self.count, 3, most)),
            pltpu.SemaphoreType.DMA((self.count,)),
            pltpu.SemaphoreType.DMA((len(self.operands),)),
        ]
        self.scratch += [pltpu.VMEM((self.rows, width), F32) for width in self.widths]
        self.scratch += [pltpu.VMEM((self.rows, width), BF16) for width in self.widths]

    def begin(self, ins, outs, scratch):
        masters, number = scratch[4 : 4 + len(self.widths)], 0
        copies = []
        for master, widths in zip(masters, self.parts):
            first = 0
            for width in widths:
                copies.append(
                    pltpu.make_async_copy(
                        ins[number], master.at[:, pl.ds(first, width)], scratch[3].at[number]
                    )
                )
                first += width
                number += 1
        for copy in copies:
            copy.start()
        return lambda: [copy.wait() for copy in copies]

    def chunks(self, place, ins, outs, scratch):
        send, recv, local = scratch[:3]
        masters = scratch[4 : 4 + len(self.widths)]
        shards = scratch[4 + len(self.widths) :]
        made, number = [], 0
        for order, plan in zip(GATHER_ORDERS, self.plan):
            group = []
            for which, columns in plan:
                group.append(
                    GatherChunk(
                        place,
                        masters[which],
                        shards[which],
                        outs[which],
                        columns,
                        order,
                        send.at[number],
                        recv.at[number],
                        local.at[number],
                    )
                )
                number += 1
            made.append(group)
        return made


class Scatter:
    held = 3

    def __init__(self, grads, dims, rows):
        self.dims, self.rows = dims, rows
        self.sources = [source for source, _, _ in grads]
        self.widths = [width for _, width, _ in grads]
        self.names = [name for _, _, name in grads] + [Name.squares]
        self.operands, self.in_specs = [], []
        self.plan = chunks_of(self.widths)
        self.count = sum(len(p) for p in self.plan)
        self.slots = slots_of(*(len(p) for p in self.plan))
        self.out_specs = [pl.BlockSpec(memory_space=pltpu.VMEM)] * len(self.names)
        self.out_shape = [jax.ShapeDtypeStruct((rows, width), F32) for width in self.widths]
        self.out_shape.append(jax.ShapeDtypeStruct((1, CHUNK), F32))
        most = max(1, max(dims) - 1)
        self.scratch = [
            pltpu.SemaphoreType.DMA((self.count, 3, most)),
            pltpu.SemaphoreType.DMA((self.count, 3, most)),
            pltpu.SemaphoreType.DMA((self.count,)),
        ]
        for order, plan in zip(SCATTER_ORDERS, self.plan):
            c, b, a = order
            rest = tuple(dims[d] for d in range(3) if d != c)
            tile, count = (rows, CHUNK), max(1, len(plan))
            self.scratch.append(pltpu.VMEM((self.held,) + rest + tile, BF16))
            for lead in (
                (max(1, dims[c] - 1),) + rest,
                (max(1, dims[b] - 1), dims[a]),
                (max(1, dims[a] - 1),),
            ):
                self.scratch.append(pltpu.VMEM((count,) + lead + tile, BF16))

    def begin(self, ins, outs, scratch):
        outs[-1][...] = jnp.zeros_like(outs[-1])
        return lambda: None

    def chunks(self, place, grads, outs, scratch):
        send, recv, local = scratch[:3]
        made, number = [], 0
        for side, (order, plan) in enumerate(zip(SCATTER_ORDERS, self.plan)):
            buffers = scratch[3 + 4 * side : 7 + 4 * side]
            group = []
            for at, (which, columns) in enumerate(plan):
                group.append(
                    ScatterChunk(
                        place,
                        grads[which],
                        outs[which],
                        outs[-1],
                        columns,
                        order,
                        buffers[0].at[at % self.held],
                        [buffer.at[at] for buffer in buffers[1:]],
                        send.at[number],
                        recv.at[number],
                        local.at[number],
                    )
                )
                number += 1
            made.append(group)
        return made


def start_row(plan, which):
    for number, row in enumerate(plan.slots):
        for order, chunk, phase in row:
            if phase == 0 and plan.plan[order][chunk][0] in which:
                return number
    return len(plan.slots)


def done_row(plan, which):
    last = 0
    for number, row in enumerate(plan.slots):
        for order, chunk, phase in row:
            if phase == 3 and plan.plan[order][chunk][0] in which:
                last = number + 1
    return last


class Phase:
    def __init__(
        self,
        body,
        grid,
        in_specs,
        out_specs,
        inputs,
        outputs,
        before=0,
        until=0,
        enter=None,
        after=None,
    ):
        self.body, self.grid, self.enter, self.after = body, grid, enter, after
        self.in_specs, self.out_specs = in_specs, out_specs
        self.inputs, self.outputs = inputs, outputs
        self.before, self.until = before, until


class Everyone:
    def __init__(self, message, held, send, recv, across):
        self.message, self.held, self.send, self.recv = message, held, send, recv
        self.tensor = lax.axis_size("tensor")
        self.across = across
        dp = lax.axis_size("dp")
        self.total = dp * self.tensor if across else dp
        self.mine = lax.axis_index("dp")
        if across:
            self.mine = self.mine * self.tensor + lax.axis_index("tensor")

    def device(self, step):
        number = lax.rem(self.mine + step, self.total)
        if not self.across:
            return {"dp": number}
        return {"dp": number // self.tensor, "tensor": lax.rem(number, self.tensor)}

    def copy(self, step, slot):
        return pltpu.make_async_remote_copy(
            src_ref=self.message,
            dst_ref=self.held.at[slot],
            send_sem=self.send.at[step],
            recv_sem=self.recv.at[step],
            device_id=self.device(step),
            device_id_type=MESH_ID,
        )

    def start(self):
        def one(step, carry):
            self.copy(step, self.mine).start()
            return carry

        lax.fori_loop(1, self.total, one, 0)
        self.held[self.mine] = self.message[...]

    def finish(self):
        def one(step, carry):
            copy = self.copy(step, lax.rem(self.mine + self.total - step, self.total))
            copy.wait_recv()
            copy.wait_send()
            return carry

        lax.fori_loop(1, self.total, one, 0)

        def add(slot, carry):
            return carry + self.held[slot]

        return lax.fori_loop(0, self.total, add, jnp.zeros(self.message.shape, F32))

    @staticmethod
    def scratch(total, rows, columns):
        return [
            pltpu.VMEM((rows, columns), F32),
            pltpu.VMEM((total, rows, columns), F32),
            pltpu.SemaphoreType.DMA((total,)),
            pltpu.SemaphoreType.DMA((total,)),
        ]


def greet_all():
    tensor = lax.axis_size("tensor")
    total = lax.axis_size("dp") * tensor
    mine = lax.axis_index("dp") * tensor + lax.axis_index("tensor")
    barrier = pltpu.get_barrier_semaphore()

    def greet(step, carry):
        number = lax.rem(mine + step, total)
        pl.semaphore_signal(
            barrier,
            inc=1,
            device_id={"dp": number // tensor, "tensor": lax.rem(number, tensor)},
            device_id_type=MESH_ID,
        )
        return carry

    lax.fori_loop(1, total, greet, 0)
    pl.semaphore_wait(barrier, total - 1)


def chain(
    name, phases, arrays, small, results, small_results, scratch, plan, collective_id, finish=None
):
    groups = [
        (False, list(arrays)),
        (False, list(small)),
        (True, len(plan.in_specs)),
        (False, list(results)),
        (False, list(small_results)),
        (True, len(plan.out_specs)),
        (False, list(scratch)),
        (True, len(plan.scratch)),
    ]

    def kernel(*everything):
        refs, lists, at = {}, [], 0
        for planned, group in groups:
            if planned:
                lists.append(list(everything[at : at + group]))
                at += group
                continue
            for label in group:
                refs[label] = everything[at]
                at += 1
        refs |= dict(zip(plan.names, lists[1]))
        place = Place(plan.dims)
        ready = plan.begin(*lists)
        if finish is None:
            entry_barrier(place)
        else:
            greet_all()
        ready()
        ins = lists[0]
        if isinstance(plan, Scatter):
            ins = [refs[source] for source in plan.sources]
        chunks = plan.chunks(place, ins, *lists[1:])

        def run(first, last):
            for row in plan.slots[first:last]:
                for order, chunk, phase in row:
                    chunks[order][chunk].act(phase)

        def find(label):
            return refs[label[0]].at[label[1]] if isinstance(label, tuple) else refs[label]

        done = 0
        for phase in phases:
            run(done, phase.before)
            done = max(done, phase.before)
            until = max(done, phase.until)
            if phase.enter is not None:
                phase.enter(refs)
            steps = math.prod(phase.grid)
            marks = [done + (until - done) * number // steps for number in range(steps + 1)]

            def body(*blocks, phase=phase, marks=marks, steps=steps):
                index = tuple(pl.program_id(axis) for axis in range(len(phase.grid)))
                step = 0
                for position, extent in zip(index, phase.grid):
                    step = step * extent + position
                for number in range(steps):
                    if marks[number] < marks[number + 1]:

                        @pl.when(step == number)
                        def _(number=number):
                            run(marks[number], marks[number + 1])

                phase.body(refs, index, *blocks)

            pltpu.emit_pipeline(
                body, grid=phase.grid, in_specs=phase.in_specs, out_specs=phase.out_specs
            )(*(find(label) for label in (*phase.inputs, *phase.outputs)))
            done = until
            if phase.after is not None:
                phase.after(refs)
        run(done, len(plan.slots))
        if finish is not None:
            finish(refs)

    in_vmem = pl.BlockSpec(memory_space=pltpu.VMEM)
    outs = pl.pallas_call(
        kernel,
        name=name,
        in_specs=[ANYWHERE] * len(arrays) + [spec for _, spec in small.values()] + plan.in_specs,
        out_specs=[ANYWHERE] * len(results) + [in_vmem] * len(small_results) + plan.out_specs,
        out_shape=[*results.values(), *small_results.values(), *plan.out_shape],
        scratch_shapes=[*scratch.values(), *plan.scratch],
        compiler_params=pltpu.CompilerParams(
            collective_id=collective_id, has_side_effects=True, vmem_limit_bytes=VMEM_BYTES
        ),
    )(*arrays.values(), *(array for array, _ in small.values()), *plan.operands)
    return dict(zip([*results, *small_results, *plan.names], outs))


def rotary_tables():
    half_size = HEAD_WIDTH // 2
    frequency = jnp.power(
        theta_base, -2.0 * jnp.arange(half_size, dtype=F32) / HEAD_WIDTH
    )
    angles = frequency[:, None] * jnp.arange(SEQUENCE_LENGTH, dtype=F32)[None, :]
    return jnp.cos(angles), jnp.sin(angles)


def rotate(values, cosine, sine, sign):
    half = HEAD_WIDTH // 2
    top, bottom = values[:half], values[half:]
    return jnp.concatenate(
        [top * cosine - sign * (bottom * sine), bottom * cosine + sign * (top * sine)], 0
    )


def product(left, right, left_dim=1, right_dim=0):
    return lax.dot_general(
        left, right, (((left_dim,), (right_dim,)), ((), ())), preferred_element_type=F32
    )


def row_scale(values):
    return lax.rsqrt(jnp.mean(values * values, -1, keepdims=True) + norm_eps)


def whole(shape):
    return pl.BlockSpec(tuple(shape), lambda *index: (0,) * len(shape))


def out_like(*shape, dtype=BF16):
    return jax.ShapeDtypeStruct(shape, dtype)


def visible(prefix, first):
    place = lax.broadcasted_iota(jnp.int32, (1, QUERY_CHUNK), 1) + first
    limit = jnp.maximum(place + 1, prefix)
    return lax.broadcasted_iota(jnp.int32, (SEQUENCE_LENGTH, QUERY_CHUNK), 0) < limit


def project_phase(tokens, width, features, full_shape, **timing):
    block = 512
    turned = features * 3 // 4
    per_sequence = SEQUENCE_LENGTH // block

    def body(refs, index, x_ref, w_ref, cos_ref, sin_ref, n_ref, out_ref):
        x = x_ref[...].astype(F32)
        normed = (x * row_scale(x) * refs[Name.gains][:1]).astype(BF16)
        n_ref[...] = normed
        raw = product(w_ref[...].reshape(width, features), normed, 0, 1)
        cosine, sine = cos_ref[...], sin_ref[...]
        for first in range(0, turned, HEAD_WIDTH):
            rows = slice(first, first + HEAD_WIDTH)
            out_ref[rows] = rotate(raw[rows], cosine, sine, 1.0).astype(BF16)
        out_ref[turned:] = raw[turned:].astype(BF16)

    table = pl.BlockSpec((HEAD_WIDTH // 2, block), lambda i: (0, lax.rem(i, per_sequence)))
    rows = pl.BlockSpec((block, width), lambda i: (i, 0))
    return Phase(
        body,
        (tokens // block,),
        [rows, whole(full_shape), table, table],
        [rows, pl.BlockSpec((features, block), lambda i: (0, i))],
        [Name.block_in, Name.qkv_full, Name.cosine, Name.sine],
        [Name.normed_one, Name.qkv],
        **timing,
    )


def attention_specs(features):
    kv_heads = features // HEAD_WIDTH // (GROUP_WIDTH + 2)
    q_heads = kv_heads * GROUP_WIDTH
    wide = (GROUP_WIDTH * HEAD_WIDTH, SEQUENCE_LENGTH)
    slim = (HEAD_WIDTH, SEQUENCE_LENGTH)
    query = pl.BlockSpec(wide, lambda s, j: (j, s))
    key = pl.BlockSpec(slim, lambda s, j: (q_heads + j, s))
    value = pl.BlockSpec(slim, lambda s, j: (q_heads + kv_heads + j, s))
    sums = pl.BlockSpec((None, GROUP_WIDTH, SEQUENCE_LENGTH), lambda s, j: (j, 0, s))
    return kv_heads, query, key, value, sums


def attend_forward_phase(tokens, features, **timing):
    kv_heads, query, key, value, sums = attention_specs(features)
    scale = SCORE_SCALE * LOG2_E

    def body(refs, index, q_ref, k_ref, v_ref, mixed_ref, sum_ref):
        prefix = refs[Name.prefix][index[0]]
        keys = k_ref[...].T
        values = jnp.concatenate([v_ref[...], jnp.ones((16, SEQUENCE_LENGTH), BF16)], 0)
        for head in range(GROUP_WIDTH):
            rows = slice(head * HEAD_WIDTH, (head + 1) * HEAD_WIDTH)
            for first in range(0, SEQUENCE_LENGTH, QUERY_CHUNK):
                columns = slice(first, first + QUERY_CHUNK)
                scores = product(keys, q_ref[rows, columns])
                scores = jnp.where(visible(prefix, first), scores, neg_fill)
                peak = jnp.max(scores, 0, keepdims=True) * scale
                weights = jnp.exp2(scores * scale - peak).astype(BF16)
                out = product(values, weights)
                total = out[HEAD_WIDTH : HEAD_WIDTH + 1]
                mixed_ref[rows, columns] = (out[:HEAD_WIDTH] * (1.0 / total)).astype(BF16)
                sum_ref[head : head + 1, columns] = peak + jnp.log2(total)

    return Phase(
        body,
        (tokens // SEQUENCE_LENGTH, kv_heads),
        [query, key, value],
        [query, sums],
        [Name.qkv, Name.qkv, Name.qkv],
        [Name.mixed, Name.logsums],
        **timing,
    )


def attend_backward_phase(tokens, features, **timing):
    kv_heads, query, key, value, sums = attention_specs(features)
    scale = SCORE_SCALE * LOG2_E

    def body(
        refs,
        index,
        q_ref,
        k_ref,
        v_ref,
        d_ref,
        mixed_ref,
        sum_ref,
        cos_ref,
        sin_ref,
        dq_ref,
        dk_ref,
        dv_ref,
    ):
        prefix = refs[Name.prefix][index[0]]
        keys_flat = k_ref[...]
        keys, values = keys_flat.T, v_ref[...].T
        dkeys = jnp.zeros((SEQUENCE_LENGTH, HEAD_WIDTH), F32)
        dvalues = jnp.zeros((SEQUENCE_LENGTH, HEAD_WIDTH), F32)
        cosine, sine = cos_ref[...], sin_ref[...]
        for head in range(GROUP_WIDTH):
            rows = slice(head * HEAD_WIDTH, (head + 1) * HEAD_WIDTH)
            for first in range(0, SEQUENCE_LENGTH, QUERY_CHUNK):
                columns = slice(first, first + QUERY_CHUNK)
                q, d = q_ref[rows, columns], d_ref[rows, columns]
                delta = jnp.sum(
                    d.astype(F32) * mixed_ref[rows, columns].astype(F32), 0, keepdims=True
                )
                scores = product(keys, q) * scale
                weights = jnp.exp2(scores - sum_ref[head : head + 1, columns])
                weights = jnp.where(visible(prefix, first), weights, 0.0)
                dweights = product(values, d)
                dscores = (weights * (dweights - delta)).astype(BF16)
                dvalues = dvalues + product(weights.astype(BF16), d.T)
                dkeys = dkeys + product(dscores, q.T)
                dq = product(keys_flat, dscores) * SCORE_SCALE
                dq_ref[rows, columns] = rotate(
                    dq, cosine[:, columns], sine[:, columns], -1.0
                ).astype(BF16)
        dk_ref[...] = rotate((dkeys * SCORE_SCALE).T, cosine, sine, -1.0).astype(BF16)
        dv_ref[...] = dvalues.T.astype(BF16)

    slim = pl.BlockSpec((HEAD_WIDTH, SEQUENCE_LENGTH), lambda s, j: (j, s))
    table = whole((HEAD_WIDTH // 2, SEQUENCE_LENGTH))
    q_features, kv_features = features // 2, features // 4
    return Phase(
        body,
        (tokens // SEQUENCE_LENGTH, kv_heads),
        [query, key, value, query, query, sums, table, table],
        [query, slim, slim],
        [Name.qkv, Name.qkv, Name.qkv, Name.dmixed, Name.mixed, Name.logsums, Name.cosine, Name.sine],
        [
            (Name.dqkv, pl.ds(0, q_features)),
            (Name.dqkv, pl.ds(q_features, kv_features)),
            (Name.dqkv, pl.ds(q_features + kv_features, kv_features)),
        ],
        **timing,
    )


def attention_out_phase(tokens, width, full_shape, **timing):
    block = 256
    features = full_shape[-1]

    def body(refs, index, mixed_ref, w_ref):
        exchange = Exchange(refs)
        rows = pl.ds(pl.multiple_of(index[0] * block, block), block)
        value = product(mixed_ref[...], w_ref[...].reshape(width, features), 0, 1)
        exchange.own[rows, :] = value.astype(BF16)
        exchange.copy(index[0], rows, pl.ds(0, width)).start()

    return Phase(
        body,
        (tokens // block,),
        [pl.BlockSpec((features, block), lambda i: (0, i)), whole(full_shape)],
        [],
        [Name.mixed, Name.o_full],
        [],
        **timing,
    )


def received(refs, index, tokens, width, wide):
    block = 256
    exchange = Exchange(refs)
    rows = pl.ds(pl.multiple_of(index * block, block), block)
    for part in range(width // wide):
        copy = exchange.copy(part * (tokens // block) + index, rows, pl.ds(part * wide, wide))
        copy.wait_recv()
        copy.wait_send()
    return exchange.own[rows, :].astype(F32) + exchange.other[rows, :].astype(F32)


def row_blocks(width):
    return pl.BlockSpec((256, width), lambda i: (i, 0))


def second_norm_phase(tokens, width, **timing):
    def body(refs, index, x_ref, middle_ref, n_ref):
        attn = received(refs, index[0], tokens, width, width)
        middle = x_ref[...].astype(F32) + attn
        middle_ref[...] = middle.astype(BF16)
        n_ref[...] = (middle * row_scale(middle) * refs[Name.gains][1:]).astype(BF16)

    rows = row_blocks(width)
    return Phase(
        body,
        (tokens // 256,),
        [rows],
        [rows, rows],
        [Name.block_in],
        [Name.middle, Name.normed_two],
        **timing,
    )


def feed_forward_phase(tokens, lead, units, **timing):
    tall, wide = 1024, 512
    width = math.prod(lead)

    def body(refs, index, n_ref, gate_w, up_w, gate_ref, up_ref, hidden_ref):
        normed = n_ref[...]
        gate = product(normed, gate_w[...].reshape(width, wide))
        up = product(normed, up_w[...].reshape(width, wide))
        gate_ref[...] = gate.astype(BF16)
        up_ref[...] = up.astype(BF16)
        hidden_ref[...] = (gate * jax.nn.sigmoid(gate) * up).astype(BF16)

    weight = pl.BlockSpec(lead + (wide,), lambda i, j: (0, 0, 0, 0, j))
    out = pl.BlockSpec((tall, wide), lambda i, j: (i, j))
    return Phase(
        body,
        (tokens // tall, units // wide),
        [pl.BlockSpec((tall, width), lambda i, j: (i, 0)), weight, weight],
        [out, out, out],
        [Name.normed_two, Name.gate_full, Name.up_full],
        [Name.gate, Name.up, Name.hidden],
        **timing,
    )


def feed_backward_phase(tokens, width, units, **timing):
    tall, wide = 512, 512

    def body(refs, index, d_ref, down_w, gate_ref, up_ref, dgate_ref, dup_ref):
        dhidden = product(d_ref[...], down_w[...])
        gate = gate_ref[...].astype(F32)
        sigmoid = jax.nn.sigmoid(gate)
        dup_ref[...] = (dhidden * gate * sigmoid).astype(BF16)
        dgate_ref[...] = (
            dhidden * up_ref[...].astype(F32) * sigmoid * (1.0 + gate * (1.0 - sigmoid))
        ).astype(BF16)

    tile = pl.BlockSpec((tall, wide), lambda i, j: (i, j))
    return Phase(
        body,
        (tokens // tall, units // wide),
        [
            pl.BlockSpec((tall, width), lambda i, j: (i, 0)),
            pl.BlockSpec((width, wide), lambda i, j: (0, j)),
            tile,
            tile,
        ],
        [tile, tile],
        [Name.out_grad, Name.down_full, Name.gate, Name.up],
        [Name.dgate, Name.dup],
        **timing,
    )


def weight_grad_phase(tokens, lead, columns, inputs, output, wide, flat=False, **timing):
    tiles = 2
    tall = math.prod(lead) // tiles

    def body(refs, index, left_ref, right_ref, out_ref):
        value = product(left_ref[...], right_ref[...], 0, 1 if flat else 0)
        out_ref[...] = value.astype(BF16).reshape(out_ref.shape)

    right = (
        pl.BlockSpec((wide, tokens), lambda i, j: (j, 0))
        if flat
        else pl.BlockSpec((tokens, wide), lambda i, j: (0, j))
    )
    out = pl.BlockSpec((lead[0] // tiles,) + lead[1:] + (wide,), lambda i, j: (i, 0, 0, 0, j))
    return Phase(
        body,
        (tiles, columns // wide),
        [pl.BlockSpec((tokens, tall), lambda i, j: (0, i)), right],
        [out],
        inputs,
        [output],
        **timing,
    )


def partial_rows_phase(tokens, width, terms, **timing):
    block, wide = 256, PARTIAL_COLUMNS

    def body(refs, index, *blocks):
        exchange = Exchange(refs)
        value = 0.0
        for number, (_, _, depth, flat) in enumerate(terms):
            left, right = blocks[2 * number : 2 * number + 2]
            value = value + product(left[...], right[...], 0 if flat else 1, 1)
        rows = pl.ds(pl.multiple_of(index[1] * block, block), block)
        columns = pl.ds(pl.multiple_of(index[0] * wide, wide), wide)
        exchange.own[rows, columns] = value.astype(BF16)
        exchange.copy(index[0] * (tokens // block) + index[1], rows, columns).start()

    specs, inputs = [], []
    for left, right, depth, flat in terms:
        specs.append(
            pl.BlockSpec((depth, block), lambda n, i: (0, i))
            if flat
            else pl.BlockSpec((block, depth), lambda n, i: (i, 0))
        )
        specs.append(pl.BlockSpec((wide, depth), lambda n, i: (n, 0)))
        inputs += [left, right]
    return Phase(body, (width // wide, tokens // block), specs, [], inputs, [], **timing)


def add_gain(refs, row, index, value):
    total = refs[Name.share_gain, 0]

    @pl.when(index == 0)
    def _():
        total[row : row + 1] = jnp.zeros_like(total[row : row + 1])

    total[row : row + 1] += jnp.sum(value, 0, keepdims=True)


def norm_back_phase(tokens, width, row, inputs, output, add, **timing):
    def body(refs, index, row_ref, back_ref, out_ref):
        dnorm = received(refs, index[0], tokens, width, PARTIAL_COLUMNS)
        values = row_ref[...].astype(F32)
        inverse = row_scale(values)
        unit = values * inverse
        add_gain(refs, row, index[0], dnorm * unit)
        change = norm_back(dnorm, refs[Name.gains][row : row + 1], unit, inverse)
        if add:
            change = change + back_ref[...].astype(F32)
        out_ref[...] = change.astype(BF16)

    rows = row_blocks(width)
    return Phase(body, (tokens // 256,), [rows, rows], [rows], inputs, [output], **timing)


def block_out_phase(tokens, width, **timing):
    def body(refs, index, middle_ref, out_ref):
        ffn = received(refs, index[0], tokens, width, PARTIAL_COLUMNS)
        out_ref[...] = (middle_ref[...].astype(F32) + ffn).astype(BF16)

    rows = row_blocks(width)
    return Phase(
        body, (tokens // 256,), [rows], [rows], [Name.middle], [Name.block_out], **timing
    )


def mixed_grad_phase(tokens, width, features, **timing):
    block = 512

    def body(refs, index, w_ref, d_ref, out_ref):
        out_ref[...] = product(w_ref[...], d_ref[...], 0, 1).astype(BF16)

    return Phase(
        body,
        (tokens // block,),
        [whole((width, features)), pl.BlockSpec((block, width), lambda i: (i, 0))],
        [pl.BlockSpec((features, block), lambda i: (0, i))],
        [Name.o_full, Name.dmiddle],
        [Name.dmixed],
        **timing,
    )


def norm_back(dnorm, gain_row, unit_rows, inverse):
    scaled = dnorm * gain_row
    return inverse * (scaled - unit_rows * jnp.mean(scaled * unit_rows, -1, keepdims=True))


def adam_step(weight, gradient, first_moment, second_moment, rate, decay, factor, fix_one, fix_two):
    clipped = factor * gradient
    first_new = beta_one * first_moment + (1.0 - beta_one) * clipped
    second_new = beta_two * second_moment + (1.0 - beta_two) * clipped * clipped
    update = first_new / fix_one / (jnp.sqrt(second_new / fix_two) + adam_eps) + decay * weight
    return (weight - rate * update, first_new, second_new)


def local(
    block_in,
    prefix_len,
    out_grad,
    step_count,
    q_weight,
    key_matrix,
    value_matrix,
    o_weight,
    gate_weight,
    up_weight,
    down_weight,
    norm_gains,
    query_mean_moment,
    key_mean_moment,
    value_mean_moment,
    output_mean_moment,
    gate_mean_moment,
    up_mean_moment,
    down_mean_moment,
    gains_mean_moment,
    q_second,
    key_square_moment,
    value_square_moment,
    o_second,
    gate_second,
    up_second,
    down_second,
    gains_second,
):
    dims = factor(lax.axis_size("dp"))
    width = block_in.shape[1]
    q_width, kv_width = q_weight.shape[1], key_matrix.shape[1]
    units = gate_weight.shape[1]
    tokens = block_in.shape[0]
    features = q_width + 2 * kv_width
    blocks = tokens // 256
    rows = q_weight.shape[0]
    lead = dims + (rows,)
    devices = lax.axis_size("dp")
    cosine, sine = rotary_tables()
    gains = (norm_gains, pl.BlockSpec(memory_space=pltpu.VMEM))
    prefix = (prefix_len, pl.BlockSpec(memory_space=pltpu.SMEM))
    per_token = out_like(tokens, width)
    per_unit = out_like(tokens, units)

    plan = Gather(
        {
            Name.qkv_full: [q_weight, key_matrix, value_matrix],
            Name.o_full: [o_weight],
            Name.gate_full: [gate_weight],
            Name.up_full: [up_weight],
            Name.down_full: [down_weight],
        },
        dims,
    )
    first = done_row(plan, (0,))
    then = done_row(plan, (1,))
    later = done_row(plan, (2, 3))
    made = chain(
        "forward",
        [
            project_phase(
                tokens, width, features, lead + (features,), before=first, until=first + 2
            ),
            attend_forward_phase(tokens, features, until=max(then, first + 8)),
            attention_out_phase(
                tokens, width, lead + (q_width,), before=then, until=(first + 8 + later) // 2
            ),
            second_norm_phase(tokens, width, until=later),
            feed_forward_phase(tokens, lead, units, before=later, until=len(plan.slots) - 2),
            weight_grad_phase(
                tokens,
                lead,
                units,
                [Name.out_grad, Name.hidden],
                Name.grad_down,
                1024,
                until=len(plan.slots),
            ),
        ],
        {
            Name.block_in: block_in,
            Name.cosine: cosine,
            Name.sine: sine,
            Name.out_grad: out_grad,
        },
        {Name.gains: gains, Name.prefix: prefix},
        {
            Name.normed_one: per_token,
            Name.qkv: out_like(features, tokens),
            Name.mixed: out_like(q_width, tokens),
            Name.logsums: out_like(kv_width // HEAD_WIDTH, GROUP_WIDTH, tokens, dtype=F32),
            Name.middle: per_token,
            Name.normed_two: per_token,
            Name.gate: per_unit,
            Name.up: per_unit,
            Name.hidden: per_unit,
            Name.grad_down: out_like(*lead, units),
        },
        {},
        Exchange.scratch(tokens, width, blocks),
        plan,
        0,
    )
    for name in (Name.qkv_full, Name.o_full, Name.gate_full, Name.up_full, Name.down_full):
        made[name] = made[name].reshape(width, -1)

    plan = Scatter(
        [
            (Name.grad_down, units, Name.sum_down),
            (Name.grad_gate, units, Name.sum_gate),
            (Name.grad_up, units, Name.sum_up),
            (Name.grad_out, q_width, Name.sum_out),
            (Name.grad_qkv, features, Name.sum_qkv),
        ],
        dims,
        rows,
    )
    gate_row, up_row, out_row, qkv_row = (start_row(plan, (which,)) for which in range(1, 5))
    last = len(plan.slots)

    def share_gains(refs):
        Everyone(*(refs[Name.share_gain, part] for part in range(4)), False).start()
        Exchange.release(refs)

    def share_squares(refs):
        refs[Name.gain_sum][...] = Everyone(
            *(refs[Name.share_gain, part] for part in range(4)), False
        ).finish()
        everyone = Everyone(*(refs[Name.share_square, part] for part in range(4)), True)
        everyone.message[...] = refs[Name.squares][...]
        everyone.start()
        refs[Name.square_sum][...] = everyone.finish()

    scratch = Exchange.scratch(tokens, width, blocks * (width // PARTIAL_COLUMNS))
    for part, kind in enumerate(Everyone.scratch(devices, 2, width)):
        scratch[Name.share_gain, part] = kind
    for part, kind in enumerate(
        Everyone.scratch(devices * lax.axis_size("tensor"), 1, CHUNK)
    ):
        scratch[Name.share_square, part] = kind
    kept = (
        Name.down_full,
        Name.gate,
        Name.up,
        Name.normed_two,
        Name.gate_full,
        Name.up_full,
        Name.middle,
        Name.o_full,
        Name.qkv,
        Name.mixed,
        Name.logsums,
        Name.normed_one,
        Name.qkv_full,
        Name.hidden,
        Name.grad_down,
    )
    made |= chain(
        "backward",
        [
            feed_backward_phase(tokens, width, units, until=gate_row // 2),
            weight_grad_phase(
                tokens,
                lead,
                units,
                [Name.normed_two, Name.dgate],
                Name.grad_gate,
                512,
                until=gate_row,
            ),
            weight_grad_phase(
                tokens,
                lead,
                units,
                [Name.normed_two, Name.dup],
                Name.grad_up,
                512,
                until=min(up_row, gate_row + 2),
            ),
            partial_rows_phase(
                tokens,
                width,
                [
                    (Name.dgate, Name.gate_full, units, False),
                    (Name.dup, Name.up_full, units, False),
                ],
                until=gate_row + 6,
            ),
            norm_back_phase(
                tokens,
                width,
                1,
                [Name.middle, Name.out_grad],
                Name.dmiddle,
                True,
                until=gate_row + 7,
                after=Exchange.release,
            ),
            mixed_grad_phase(tokens, width, q_width, until=gate_row + 8),
            weight_grad_phase(
                tokens,
                lead,
                q_width,
                [Name.dmiddle, Name.mixed],
                Name.grad_out,
                q_width,
                flat=True,
                until=out_row,
            ),
            attend_backward_phase(tokens, features, until=qkv_row),
            weight_grad_phase(
                tokens, lead, features, [Name.normed_one, Name.dqkv], Name.grad_qkv, 768, flat=True
            ),
            partial_rows_phase(
                tokens,
                width,
                [(Name.dqkv, Name.qkv_full, features, True)],
                until=qkv_row + 3,
                enter=Exchange.claim,
            ),
            norm_back_phase(
                tokens,
                width,
                0,
                [Name.block_in, Name.dmiddle],
                Name.change,
                False,
                until=qkv_row + 4,
                after=share_gains,
            ),
            partial_rows_phase(
                tokens,
                width,
                [(Name.hidden, Name.down_full, units, False)],
                until=qkv_row + 7,
                enter=Exchange.claim,
            ),
            block_out_phase(tokens, width, until=qkv_row + 8),
        ],
        {
            Name.out_grad: out_grad,
            Name.block_in: block_in,
            Name.cosine: cosine,
            Name.sine: sine,
        }
        | {name: made[name] for name in kept},
        {Name.gains: gains, Name.prefix: prefix},
        {
            Name.dgate: per_unit,
            Name.dup: per_unit,
            Name.grad_gate: out_like(*lead, units),
            Name.grad_up: out_like(*lead, units),
            Name.dmiddle: per_token,
            Name.dmixed: out_like(q_width, tokens),
            Name.grad_out: out_like(*lead, q_width),
            Name.dqkv: out_like(features, tokens),
            Name.grad_qkv: out_like(*lead, features),
            Name.change: per_token,
            Name.block_out: per_token,
        },
        {
            Name.gain_sum: out_like(2, width, dtype=F32),
            Name.square_sum: out_like(1, CHUNK, dtype=F32),
        },
        scratch,
        plan,
        1,
        share_squares,
    )
    sum_qkv, sum_out, sum_gate, sum_up, sum_down = (
        made[name]
        for name in (Name.sum_qkv, Name.sum_out, Name.sum_gate, Name.sum_up, Name.sum_down)
    )
    block_out = made[Name.block_out]
    in_grad = made[Name.dmiddle].astype(F32) + made[Name.change].astype(F32)
    gain_sum = made[Name.gain_sum]
    total_square = jnp.sum(made[Name.square_sum]) + jnp.sum(jnp.square(gain_sum))
    gain_width = width // devices
    first_column = lax.axis_index("dp") * gain_width
    grad_gains = lax.dynamic_slice_in_dim(gain_sum, first_column, gain_width, 1)
    old_gains = lax.dynamic_slice_in_dim(norm_gains, first_column, gain_width, 1)
    reduced = (
        sum_qkv[:, :q_width],
        sum_qkv[:, q_width : q_width + kv_width],
        sum_qkv[:, q_width + kv_width :],
        sum_out,
        sum_gate,
        sum_up,
        sum_down,
        grad_gains,
    )
    grad_norm = jnp.sqrt(total_square)
    factor_now = jnp.minimum(1.0, clip_limit / grad_norm)
    step_float = step_count[0].astype(F32)
    fix_one = 1.0 - jnp.power(beta_one, step_float)
    fix_two = 1.0 - jnp.power(beta_two, step_float)
    masters = (
        q_weight,
        key_matrix,
        value_matrix,
        o_weight,
        gate_weight,
        up_weight,
        down_weight,
        old_gains,
    )
    firsts = (
        query_mean_moment,
        key_mean_moment,
        value_mean_moment,
        output_mean_moment,
        gate_mean_moment,
        up_mean_moment,
        down_mean_moment,
        gains_mean_moment,
    )
    seconds = (
        q_second,
        key_square_moment,
        value_square_moment,
        o_second,
        gate_second,
        up_second,
        down_second,
        gains_second,
    )
    rate_list = matrix_rates + (gain_rate,)
    decay_list = (decay_rate,) * 7 + (0.0,)
    new_weights, new_firsts, new_seconds = ([], [], [])
    for weight, gradient, first_moment, second_moment, rate, decay in zip(
        masters, reduced, firsts, seconds, rate_list, decay_list
    ):
        weight_new, first_new, second_new = adam_step(
            weight, gradient, first_moment, second_moment, rate, decay, factor_now, fix_one, fix_two
        )
        new_weights.append(weight_new)
        new_firsts.append(first_new)
        new_seconds.append(second_new)
    return (
        block_out,
        in_grad,
        grad_norm.reshape(1),
        new_weights[0],
        new_weights[1],
        new_weights[2],
        new_weights[3],
        new_weights[4],
        new_weights[5],
        new_weights[6],
        new_weights[7],
        new_firsts[0],
        new_firsts[1],
        new_firsts[2],
        new_firsts[3],
        new_firsts[4],
        new_firsts[5],
        new_firsts[6],
        new_firsts[7],
        new_seconds[0],
        new_seconds[1],
        new_seconds[2],
        new_seconds[3],
        new_seconds[4],
        new_seconds[5],
        new_seconds[6],
        new_seconds[7],
    )


def solution(mesh):
    return jax.shard_map(
        local,
        mesh=mesh,
        in_specs=(
            P("dp", None),
            P("dp"),
            P("dp", None),
            P(),
            P("dp", "tensor"),
            P("dp", "tensor"),
            P("dp", "tensor"),
            P("dp", "tensor"),
            P("dp", "tensor"),
            P("dp", "tensor"),
            P("dp", "tensor"),
            P(),
            P("dp", "tensor"),
            P("dp", "tensor"),
            P("dp", "tensor"),
            P("dp", "tensor"),
            P("dp", "tensor"),
            P("dp", "tensor"),
            P("dp", "tensor"),
            P(None, "dp"),
            P("dp", "tensor"),
            P("dp", "tensor"),
            P("dp", "tensor"),
            P("dp", "tensor"),
            P("dp", "tensor"),
            P("dp", "tensor"),
            P("dp", "tensor"),
            P(None, "dp"),
        ),
        out_specs=(
            P("dp", None),
            P("dp", None),
            P(),
            P("dp", "tensor"),
            P("dp", "tensor"),
            P("dp", "tensor"),
            P("dp", "tensor"),
            P("dp", "tensor"),
            P("dp", "tensor"),
            P("dp", "tensor"),
            P(None, "dp"),
            P("dp", "tensor"),
            P("dp", "tensor"),
            P("dp", "tensor"),
            P("dp", "tensor"),
            P("dp", "tensor"),
            P("dp", "tensor"),
            P("dp", "tensor"),
            P(None, "dp"),
            P("dp", "tensor"),
            P("dp", "tensor"),
            P("dp", "tensor"),
            P("dp", "tensor"),
            P("dp", "tensor"),
            P("dp", "tensor"),
            P("dp", "tensor"),
            P(None, "dp"),
        ),
        check_vma=False,
    )
```

```python
import enum
import math

import jax
import jax.numpy as jnp
from jax import lax
from jax.experimental import pallas as pl
from jax.experimental.pallas import tpu as pltpu
from jax.sharding import PartitionSpec as P

HEAD_WIDTH = 96
GROUP_WIDTH = 2
SEQUENCE_LENGTH = 1024
QUERY_CHUNK = 512
VMEM_BYTES = 62 * 2**20
LOG2_E = 1.4426950408889634
SCORE_SCALE = 1.0 / math.sqrt(HEAD_WIDTH)

theta_base = 100000.0
norm_eps = 1e-05
beta_one = 0.9
beta_two = 0.95
adam_eps = 1e-08
decay_rate = 0.1
clip_limit = 1.0
neg_fill = -1e30
matrix_rates = (0.08, 0.08, 0.08, 1.0, 0.08, 0.08, 0.1)
gain_rate = 1.0

BF16 = jnp.bfloat16
F32 = jnp.float32
ANYWHERE = pl.BlockSpec(memory_space=pl.ANY)
MESH_ID = pl.DeviceIdType.MESH
GATHER_ORDERS = ((0, 1, 2), (2, 0, 1))
SCATTER_ORDERS = ((2, 1, 0), (1, 0, 2))
CHUNK = 256
PARTIAL_COLUMNS = 512


class Name(enum.Enum):
    block_in = enum.auto()
    block_out = enum.auto()
    in_grad = enum.auto()
    cosine = enum.auto()
    dgate = enum.auto()
    dmiddle = enum.auto()
    dmixed = enum.auto()
    down_full = enum.auto()
    dqkv = enum.auto()
    dup = enum.auto()
    gain_sum = enum.auto()
    gains = enum.auto()
    gate = enum.auto()
    gate_full = enum.auto()
    grad_down = enum.auto()
    grad_gate = enum.auto()
    grad_out = enum.auto()
    grad_qkv = enum.auto()
    grad_up = enum.auto()
    hidden = enum.auto()
    logsums = enum.auto()
    middle = enum.auto()
    mixed = enum.auto()
    normed_one = enum.auto()
    normed_two = enum.auto()
    o_full = enum.auto()
    out_grad = enum.auto()
    prefix = enum.auto()
    qkv = enum.auto()
    qkv_full = enum.auto()
    share_gain = enum.auto()
    share_square = enum.auto()
    sine = enum.auto()
    square_sum = enum.auto()
    squares = enum.auto()
    sum_down = enum.auto()
    sum_gate = enum.auto()
    sum_out = enum.auto()
    sum_qkv = enum.auto()
    sum_up = enum.auto()
    swap = enum.auto()
    up = enum.auto()
    up_full = enum.auto()


def factor(count):
    return {16: (4, 2, 2), 64: (4, 4, 4)}.get(count, (count, 1, 1))


class Place:
    def __init__(self, dims):
        self.dims = dims
        mine = lax.axis_index("dp")
        n0, n1, n2 = dims
        self.at = (lax.rem(mine // (n1 * n2), n0), lax.rem(mine // n2, n1), lax.rem(mine, n2))

    def peer(self, dim, step):
        return lax.rem(self.at[dim] + step, self.dims[dim])

    def device(self, dim, coord):
        digits = list(self.at)
        digits[dim] = coord
        return {"dp": (digits[0] * self.dims[1] + digits[1]) * self.dims[2] + digits[2]}


def view(ref, fixed, columns):
    picks = tuple(fixed.get(d, slice(None)) for d in range(3))
    return ref.at[picks + (slice(None), pl.ds(columns[0], columns[1]))]


def entry_barrier(place):
    barrier = pltpu.get_barrier_semaphore()
    total = 0
    for dim in range(3):
        for step in range(1, place.dims[dim]):
            pl.semaphore_signal(
                barrier,
                inc=1,
                device_id=place.device(dim, place.peer(dim, step)),
                device_id_type=MESH_ID,
            )
            total += 1
    pl.semaphore_signal(
        barrier, inc=1, device_id={"tensor": 1 - lax.axis_index("tensor")}, device_id_type=MESH_ID
    )
    pl.semaphore_wait(barrier, total + 1)


class Exchange:
    def __init__(self, refs):
        self.own, self.other, self.send, self.recv, self.free = (
            refs[Name.swap, part] for part in range(5)
        )
        self.peer = {"tensor": 1 - lax.axis_index("tensor")}

    def copy(self, number, rows, columns):
        return pltpu.make_async_remote_copy(
            src_ref=self.own.at[rows, columns],
            dst_ref=self.other.at[rows, columns],
            send_sem=self.send.at[number],
            recv_sem=self.recv.at[number],
            device_id=self.peer,
            device_id_type=MESH_ID,
        )

    @staticmethod
    def release(refs):
        here = Exchange(refs)
        pl.semaphore_signal(here.free, inc=1, device_id=here.peer, device_id_type=MESH_ID)

    @staticmethod
    def claim(refs):
        pl.semaphore_wait(refs[Name.swap, 4], 1)

    @staticmethod
    def scratch(tokens, width, count):
        kinds = (
            pltpu.VMEM((tokens, width), BF16),
            pltpu.VMEM((tokens, width), BF16),
            pltpu.SemaphoreType.DMA((count,)),
            pltpu.SemaphoreType.DMA((count,)),
            pltpu.SemaphoreType.REGULAR,
        )
        return {(Name.swap, part): kind for part, kind in enumerate(kinds)}


class GatherChunk:
    def __init__(self, place, master, shard, full, columns, order, send, recv, local):
        self.place, self.shard, self.full, self.columns = place, shard, full, columns
        self.order, self.send, self.recv, self.local = order, send, recv, local
        self.master = master

    def copies(self, stage, arriving):
        place, dim, made = self.place, self.order[stage], []
        for step in range(1, place.dims[dim]):
            fixed = {d: place.at[d] for d in self.order[stage:]}
            if arriving:
                fixed[dim] = place.peer(dim, place.dims[dim] - step)
            target = view(self.full, fixed, self.columns)
            source = target
            if stage == 0 and not arriving:
                source = self.shard.at[:, pl.ds(*self.columns)]
            made.append(
                pltpu.make_async_remote_copy(
                    src_ref=source,
                    dst_ref=target,
                    send_sem=self.send.at[stage, step - 1],
                    recv_sem=self.recv.at[stage, step - 1],
                    device_id=place.device(dim, place.peer(dim, step)),
                    device_id_type=MESH_ID,
                )
            )
        return made

    def own(self):
        fixed = {d: self.place.at[d] for d in range(3)}
        return pltpu.make_async_copy(
            self.shard.at[:, pl.ds(*self.columns)],
            view(self.full, fixed, self.columns),
            self.local,
        )

    def act(self, phase):
        if phase == 0:
            columns = slice(self.columns[0], self.columns[0] + self.columns[1])
            self.shard[:, columns] = self.master[:, columns].astype(BF16)
            self.own().start()
        else:
            if phase == 1:
                self.own().wait()
            for copy in self.copies(phase - 1, True):
                copy.wait_recv()
        if phase < 3:
            for copy in self.copies(phase, False):
                copy.start()
        else:
            for stage in range(3):
                for copy in self.copies(stage, False):
                    copy.wait_send()


class ScatterChunk:
    def __init__(
        self, place, grad, out, squares, columns, order, mine, landings, send, recv, local
    ):
        self.place, self.grad, self.out, self.columns = place, grad, out, columns
        self.order, self.send, self.recv, self.local = order, send, recv, local
        self.squares, self.mine, self.landings = squares, mine, landings
        self.total = landings[0].at[0]
        self.rest = [d for d in range(3) if d != order[0]]

    def pick(self, second, third):
        return tuple(second if d == self.order[1] else third for d in self.rest)

    def copies(self, stage, arriving):
        place, dim, made = self.place, self.order[stage], []
        for step in range(1, place.dims[dim]):
            to = place.peer(dim, step)
            land = self.landings[stage].at[step - 1]
            if arriving:
                source = land
            elif stage == 0:
                source = view(self.grad, {dim: to}, self.columns)
            elif stage == 1:
                source = self.total.at[self.pick(to, slice(None))]
            else:
                source = self.total.at[self.pick(place.at[self.order[1]], to)]
            made.append(
                pltpu.make_async_remote_copy(
                    src_ref=source,
                    dst_ref=land,
                    send_sem=self.send.at[stage, step - 1],
                    recv_sem=self.recv.at[stage, step - 1],
                    device_id=place.device(dim, to),
                    device_id_type=MESH_ID,
                )
            )
        return made

    def own(self):
        first = self.order[0]
        return pltpu.make_async_copy(
            view(self.grad, {first: self.place.at[first]}, self.columns), self.mine, self.local
        )

    def add(self, target, value, landing, stage):
        slots = self.place.dims[self.order[stage]] - 1
        if slots == 1:
            target[...] = value + landing[0]
        elif slots > 1:
            value = value.astype(F32)
            for slot in range(slots):
                value = value + landing[slot].astype(F32)
            target[...] = value.astype(BF16)
        else:
            target[...] = value

    def act(self, phase):
        place, order = self.place, self.order
        if phase == 0:
            self.own().start()
        else:
            for copy in self.copies(phase - 1, True):
                copy.wait_recv()
        if phase == 1:
            self.own().wait()
            self.add(self.total, self.mine[...], self.landings[0], 0)
        if phase == 2:
            spot = self.total.at[self.pick(place.at[order[1]], slice(None))]
            self.add(spot, spot[...], self.landings[1], 1)
        if phase < 3:
            for copy in self.copies(phase, False):
                copy.start()
        else:
            value = self.total[self.pick(place.at[order[1]], place.at[order[2]])].astype(F32)
            for slot in range(place.dims[order[2]] - 1):
                value = value + self.landings[2][slot].astype(F32)
            self.out[:, self.columns[0] : self.columns[0] + self.columns[1]] = value
            self.squares[...] += jnp.sum(value * value, 0, keepdims=True)
            for stage in range(3):
                for copy in self.copies(stage, False):
                    copy.wait_send()


def chunks_of(widths):
    first, second = [], []
    for which, width in enumerate(widths):
        count = width // CHUNK
        later = max(1, round(count * 4 / 11))
        for i in range(count):
            (first if i < count - later else second).append((which, (i * CHUNK, CHUNK)))
    return first, second


def woven(plan, pair):
    first, second = ([c for c in side if c[0] not in pair] for side in plan)
    count = sum(len(side) for side in plan) - len(first) - len(second)
    later = [3, 5, 7] if count == 16 else list(range(count // 2 - 1, 0, -3))
    chunks = [(which, (i * CHUNK, CHUNK)) for i in range(count // 2) for which in pair]
    for side, keep in ((first, False), (second, True)):
        at = sum(1 for which, _ in side if which < pair[0])
        side[at:at] = [c for c in chunks if (c[1][0] // CHUNK in later) == keep]
    return first, second


def slots_of(first, second, stride=2):
    rows = []
    for slot in range(max(first, second) + 3 * stride):
        row = []
        for phase in (3, 2, 1, 0):
            if 0 <= slot - phase * stride < first:
                row.append((0, slot - phase * stride, phase))
            for chunk in range(second):
                if round(chunk * max(1, first) / max(1, second)) + phase * stride == slot:
                    row.append((1, chunk, phase))
        rows.append(row)
    return rows


class Gather:
    def __init__(self, shards, dims, pair):
        self.dims, self.names = dims, list(shards)
        self.parts = [[part.shape[1] for part in parts] for parts in shards.values()]
        self.operands = [part for parts in shards.values() for part in parts]
        self.widths = [sum(widths) for widths in self.parts]
        self.rows = self.operands[0].shape[0]
        self.plan = woven(chunks_of(self.widths), pair)
        self.count = sum(len(p) for p in self.plan)
        self.slots = slots_of(*(len(p) for p in self.plan))
        self.in_specs = [ANYWHERE] * len(self.operands)
        self.out_specs = [ANYWHERE] * len(shards)
        self.out_shape = [
            jax.ShapeDtypeStruct(dims + (self.rows, width), BF16) for width in self.widths
        ]
        most = max(1, max(dims) - 1)
        self.scratch = [
            pltpu.SemaphoreType.DMA((self.count, 3, most)),
            pltpu.SemaphoreType.DMA((self.count, 3, most)),
            pltpu.SemaphoreType.DMA((self.count,)),
            pltpu.SemaphoreType.DMA((len(self.operands),)),
        ]
        self.scratch += [pltpu.VMEM((self.rows, width), F32) for width in self.widths]
        self.scratch += [pltpu.VMEM((self.rows, width), BF16) for width in self.widths]

    def begin(self, ins, outs, scratch):
        masters, number = scratch[4 : 4 + len(self.widths)], 0
        copies = []
        for master, widths in zip(masters, self.parts):
            first = 0
            for width in widths:
                copies.append(
                    pltpu.make_async_copy(
                        ins[number], master.at[:, pl.ds(first, width)], scratch[3].at[number]
                    )
                )
                first += width
                number += 1
        for copy in copies:
            copy.start()
        return lambda: [copy.wait() for copy in copies]

    def chunks(self, place, ins, outs, scratch):
        send, recv, local = scratch[:3]
        masters = scratch[4 : 4 + len(self.widths)]
        shards = scratch[4 + len(self.widths) :]
        made, number = [], 0
        for order, plan in zip(GATHER_ORDERS, self.plan):
            group = []
            for which, columns in plan:
                group.append(
                    GatherChunk(
                        place,
                        masters[which],
                        shards[which],
                        outs[which],
                        columns,
                        order,
                        send.at[number],
                        recv.at[number],
                        local.at[number],
                    )
                )
                number += 1
            made.append(group)
        return made


class Scatter:
    held = 3

    def __init__(self, grads, dims, rows):
        self.dims, self.rows = dims, rows
        self.sources = [source for source, _, _ in grads]
        self.widths = [width for _, width, _ in grads]
        self.names = [name for _, _, name in grads] + [Name.squares]
        self.operands, self.in_specs = [], []
        self.plan = chunks_of(self.widths)
        self.count = sum(len(p) for p in self.plan)
        self.slots = slots_of(*(len(p) for p in self.plan))
        self.out_specs = [pl.BlockSpec(memory_space=pltpu.VMEM)] * len(self.names)
        self.out_shape = [jax.ShapeDtypeStruct((rows, width), F32) for width in self.widths]
        self.out_shape.append(jax.ShapeDtypeStruct((1, CHUNK), F32))
        most = max(1, max(dims) - 1)
        self.scratch = [
            pltpu.SemaphoreType.DMA((self.count, 3, most)),
            pltpu.SemaphoreType.DMA((self.count, 3, most)),
            pltpu.SemaphoreType.DMA((self.count,)),
        ]
        for order, plan in zip(SCATTER_ORDERS, self.plan):
            c, b, a = order
            rest = tuple(dims[d] for d in range(3) if d != c)
            tile, count = (rows, CHUNK), max(1, len(plan))
            self.scratch.append(pltpu.VMEM((self.held,) + rest + tile, BF16))
            for lead in (
                (max(1, dims[c] - 1),) + rest,
                (max(1, dims[b] - 1), dims[a]),
                (max(1, dims[a] - 1),),
            ):
                self.scratch.append(pltpu.VMEM((count,) + lead + tile, BF16))

    def begin(self, ins, outs, scratch):
        outs[-1][...] = jnp.zeros_like(outs[-1])
        return lambda: None

    def chunks(self, place, grads, outs, scratch):
        send, recv, local = scratch[:3]
        made, number = [], 0
        for side, (order, plan) in enumerate(zip(SCATTER_ORDERS, self.plan)):
            buffers = scratch[3 + 4 * side : 7 + 4 * side]
            group = []
            for at, (which, columns) in enumerate(plan):
                group.append(
                    ScatterChunk(
                        place,
                        grads[which],
                        outs[which],
                        outs[-1],
                        columns,
                        order,
                        buffers[0].at[at % self.held],
                        [buffer.at[at] for buffer in buffers[1:]],
                        send.at[number],
                        recv.at[number],
                        local.at[number],
                    )
                )
                number += 1
            made.append(group)
        return made


def start_row(plan, which):
    for number, row in enumerate(plan.slots):
        for order, chunk, phase in row:
            if phase == 0 and plan.plan[order][chunk][0] in which:
                return number
    return len(plan.slots)


def done_row(plan, which, end=None):
    last = 0
    for number, row in enumerate(plan.slots):
        for order, chunk, phase in row:
            array, (column, _) = plan.plan[order][chunk]
            if phase == 3 and array in which and (end is None or column < end):
                last = number + 1
    return last


class Phase:
    def __init__(
        self,
        body,
        grid,
        in_specs,
        out_specs,
        inputs,
        outputs,
        before=0,
        until=0,
        enter=None,
        after=None,
        marks=None,
    ):
        self.body, self.grid, self.enter, self.after = body, grid, enter, after
        self.marks = marks
        self.in_specs, self.out_specs = in_specs, out_specs
        self.inputs, self.outputs = inputs, outputs
        self.before, self.until = before, until


class Everyone:
    def __init__(self, message, held, send, recv, across):
        self.message, self.held, self.send, self.recv = message, held, send, recv
        self.tensor = lax.axis_size("tensor")
        self.across = across
        dp = lax.axis_size("dp")
        self.total = dp * self.tensor if across else dp
        self.mine = lax.axis_index("dp")
        if across:
            self.mine = self.mine * self.tensor + lax.axis_index("tensor")

    def device(self, step):
        number = lax.rem(self.mine + step, self.total)
        if not self.across:
            return {"dp": number}
        return {"dp": number // self.tensor, "tensor": lax.rem(number, self.tensor)}

    def copy(self, step, slot):
        return pltpu.make_async_remote_copy(
            src_ref=self.message,
            dst_ref=self.held.at[slot],
            send_sem=self.send.at[step],
            recv_sem=self.recv.at[step],
            device_id=self.device(step),
            device_id_type=MESH_ID,
        )

    def start(self):
        def one(step, carry):
            self.copy(step, self.mine).start()
            return carry

        lax.fori_loop(1, self.total, one, 0)
        self.held[self.mine] = self.message[...]

    def finish(self):
        def one(step, carry):
            copy = self.copy(step, lax.rem(self.mine + self.total - step, self.total))
            copy.wait_recv()
            copy.wait_send()
            return carry

        lax.fori_loop(1, self.total, one, 0)

        def add(slot, carry):
            return carry + self.held[slot]

        return lax.fori_loop(0, self.total, add, jnp.zeros(self.message.shape, F32))

    @staticmethod
    def scratch(total, rows, columns):
        return [
            pltpu.VMEM((rows, columns), F32),
            pltpu.VMEM((total, rows, columns), F32),
            pltpu.SemaphoreType.DMA((total,)),
            pltpu.SemaphoreType.DMA((total,)),
        ]


def greet_all():
    tensor = lax.axis_size("tensor")
    total = lax.axis_size("dp") * tensor
    mine = lax.axis_index("dp") * tensor + lax.axis_index("tensor")
    barrier = pltpu.get_barrier_semaphore()

    def greet(step, carry):
        number = lax.rem(mine + step, total)
        pl.semaphore_signal(
            barrier,
            inc=1,
            device_id={"dp": number // tensor, "tensor": lax.rem(number, tensor)},
            device_id_type=MESH_ID,
        )
        return carry

    lax.fori_loop(1, total, greet, 0)
    pl.semaphore_wait(barrier, total - 1)


def chain(
    name, phases, arrays, small, results, small_results, scratch, plan, collective_id, finish=None
):
    groups = [
        (False, list(arrays)),
        (False, list(small)),
        (True, len(plan.in_specs)),
        (False, list(results)),
        (False, list(small_results)),
        (True, len(plan.out_specs)),
        (False, list(scratch)),
        (True, len(plan.scratch)),
    ]

    def kernel(*everything):
        refs, lists, at = {}, [], 0
        for planned, group in groups:
            if planned:
                lists.append(list(everything[at : at + group]))
                at += group
                continue
            for label in group:
                refs[label] = everything[at]
                at += 1
        refs |= dict(zip(plan.names, lists[1]))
        place = Place(plan.dims)
        ready = plan.begin(*lists)
        if finish is None:
            entry_barrier(place)
        else:
            greet_all()
        ready()
        ins = lists[0]
        if isinstance(plan, Scatter):
            ins = [refs[source] for source in plan.sources]
        chunks = plan.chunks(place, ins, *lists[1:])

        def run(first, last):
            for row in plan.slots[first:last]:
                for order, chunk, phase in row:
                    chunks[order][chunk].act(phase)

        def find(label):
            return refs[label[0]].at[label[1]] if isinstance(label, tuple) else refs[label]

        done = 0
        for phase in phases:
            run(done, phase.before)
            done = max(done, phase.before)
            until = max(done, phase.until)
            if phase.enter is not None:
                phase.enter(refs)
            steps = math.prod(phase.grid)
            marks = [done + (until - done) * number // steps for number in range(steps + 1)]
            if phase.marks is not None:
                marks = [done, *(max(done, mark) for mark in phase.marks)]
                until = marks[-1]

            def body(*blocks, phase=phase, marks=marks, steps=steps):
                index = tuple(pl.program_id(axis) for axis in range(len(phase.grid)))
                step = 0
                for position, extent in zip(index, phase.grid):
                    step = step * extent + position
                if phase.marks is not None:
                    phase.body(refs, index, *blocks)
                for number in range(steps):
                    if marks[number] < marks[number + 1]:

                        @pl.when(step == number)
                        def _(number=number):
                            run(marks[number], marks[number + 1])

                if phase.marks is None:
                    phase.body(refs, index, *blocks)

            pltpu.emit_pipeline(
                body, grid=phase.grid, in_specs=phase.in_specs, out_specs=phase.out_specs
            )(*(find(label) for label in (*phase.inputs, *phase.outputs)))
            done = until
            if phase.after is not None:
                phase.after(refs)
        run(done, len(plan.slots))
        if finish is not None:
            finish(refs)

    in_vmem = pl.BlockSpec(memory_space=pltpu.VMEM)
    outs = pl.pallas_call(
        kernel,
        name=name,
        in_specs=[ANYWHERE] * len(arrays) + [spec for _, spec in small.values()] + plan.in_specs,
        out_specs=[ANYWHERE] * len(results) + [in_vmem] * len(small_results) + plan.out_specs,
        out_shape=[*results.values(), *small_results.values(), *plan.out_shape],
        scratch_shapes=[*scratch.values(), *plan.scratch],
        compiler_params=pltpu.CompilerParams(
            collective_id=collective_id, has_side_effects=True, vmem_limit_bytes=VMEM_BYTES
        ),
    )(*arrays.values(), *(array for array, _ in small.values()), *plan.operands)
    return dict(zip([*results, *small_results, *plan.names], outs))


def rotary_tables():
    half_size = HEAD_WIDTH // 2
    frequency = jnp.power(
        theta_base, -2.0 * jnp.arange(half_size, dtype=F32) / HEAD_WIDTH
    )
    angles = frequency[:, None] * jnp.arange(SEQUENCE_LENGTH, dtype=F32)[None, :]
    return jnp.cos(angles), jnp.sin(angles)


def rotate(values, cosine, sine, sign):
    half = HEAD_WIDTH // 2
    top, bottom = values[:half], values[half:]
    return jnp.concatenate(
        [top * cosine - sign * (bottom * sine), bottom * cosine + sign * (top * sine)], 0
    )


def product(left, right, left_dim=1, right_dim=0):
    return lax.dot_general(
        left, right, (((left_dim,), (right_dim,)), ((), ())), preferred_element_type=F32
    )


def row_scale(values):
    return lax.rsqrt(jnp.mean(values * values, -1, keepdims=True) + norm_eps)


def whole(shape):
    return pl.BlockSpec(tuple(shape), lambda *index: (0,) * len(shape))


def out_like(*shape, dtype=BF16):
    return jax.ShapeDtypeStruct(shape, dtype)


def visible(prefix, first):
    place = lax.broadcasted_iota(jnp.int32, (1, QUERY_CHUNK), 1) + first
    limit = jnp.maximum(place + 1, prefix)
    return lax.broadcasted_iota(jnp.int32, (SEQUENCE_LENGTH, QUERY_CHUNK), 0) < limit


def project_phase(tokens, width, features, full_shape, **timing):
    block = 512
    turned = features * 3 // 4
    per_sequence = SEQUENCE_LENGTH // block

    def body(refs, index, x_ref, w_ref, cos_ref, sin_ref, n_ref, out_ref):
        x = x_ref[...].astype(F32)
        normed = (x * row_scale(x) * refs[Name.gains][:1]).astype(BF16)
        n_ref[...] = normed
        raw = product(w_ref[...].reshape(width, features), normed, 0, 1)
        cosine, sine = cos_ref[...], sin_ref[...]
        for first in range(0, turned, HEAD_WIDTH):
            rows = slice(first, first + HEAD_WIDTH)
            out_ref[rows] = rotate(raw[rows], cosine, sine, 1.0).astype(BF16)
        out_ref[turned:] = raw[turned:].astype(BF16)

    table = pl.BlockSpec((HEAD_WIDTH // 2, block), lambda i: (0, lax.rem(i, per_sequence)))
    rows = pl.BlockSpec((block, width), lambda i: (i, 0))
    return Phase(
        body,
        (tokens // block,),
        [rows, whole(full_shape), table, table],
        [rows, pl.BlockSpec((features, block), lambda i: (0, i))],
        [Name.block_in, Name.qkv_full, Name.cosine, Name.sine],
        [Name.normed_one, Name.qkv],
        **timing,
    )


def attention_specs(features):
    kv_heads = features // HEAD_WIDTH // (GROUP_WIDTH + 2)
    q_heads = kv_heads * GROUP_WIDTH
    wide = (GROUP_WIDTH * HEAD_WIDTH, SEQUENCE_LENGTH)
    slim = (HEAD_WIDTH, SEQUENCE_LENGTH)
    query = pl.BlockSpec(wide, lambda s, j: (j, s))
    key = pl.BlockSpec(slim, lambda s, j: (q_heads + j, s))
    value = pl.BlockSpec(slim, lambda s, j: (q_heads + kv_heads + j, s))
    sums = pl.BlockSpec((None, GROUP_WIDTH, SEQUENCE_LENGTH), lambda s, j: (j, 0, s))
    return kv_heads, query, key, value, sums


def attend_forward_phase(tokens, features, **timing):
    kv_heads, query, key, value, sums = attention_specs(features)
    scale = SCORE_SCALE * LOG2_E

    def body(refs, index, q_ref, k_ref, v_ref, mixed_ref, sum_ref):
        prefix = refs[Name.prefix][index[0]]
        keys = k_ref[...].T
        values = jnp.concatenate([v_ref[...], jnp.ones((16, SEQUENCE_LENGTH), BF16)], 0)
        for head in range(GROUP_WIDTH):
            rows = slice(head * HEAD_WIDTH, (head + 1) * HEAD_WIDTH)
            for first in range(0, SEQUENCE_LENGTH, QUERY_CHUNK):
                columns = slice(first, first + QUERY_CHUNK)
                scores = product(keys, q_ref[rows, columns])
                scores = jnp.where(visible(prefix, first), scores, neg_fill)
                peak = jnp.max(scores, 0, keepdims=True) * scale
                weights = jnp.exp2(scores * scale - peak).astype(BF16)
                out = product(values, weights)
                total = out[HEAD_WIDTH : HEAD_WIDTH + 1]
                mixed_ref[rows, columns] = (out[:HEAD_WIDTH] * (1.0 / total)).astype(BF16)
                sum_ref[head : head + 1, columns] = peak + jnp.log2(total)

    return Phase(
        body,
        (tokens // SEQUENCE_LENGTH, kv_heads),
        [query, key, value],
        [query, sums],
        [Name.qkv, Name.qkv, Name.qkv],
        [Name.mixed, Name.logsums],
        **timing,
    )


def attend_backward_phase(tokens, features, **timing):
    kv_heads, query, key, value, sums = attention_specs(features)
    scale = SCORE_SCALE * LOG2_E

    def body(
        refs,
        index,
        q_ref,
        k_ref,
        v_ref,
        d_ref,
        mixed_ref,
        sum_ref,
        cos_ref,
        sin_ref,
        dq_ref,
        dk_ref,
        dv_ref,
    ):
        prefix = refs[Name.prefix][index[0]]
        keys_flat = k_ref[...]
        keys, values = keys_flat.T, v_ref[...].T
        dkeys = jnp.zeros((SEQUENCE_LENGTH, HEAD_WIDTH), F32)
        dvalues = jnp.zeros((SEQUENCE_LENGTH, HEAD_WIDTH), F32)
        cosine, sine = cos_ref[...], sin_ref[...]
        for head in range(GROUP_WIDTH):
            rows = slice(head * HEAD_WIDTH, (head + 1) * HEAD_WIDTH)
            for first in range(0, SEQUENCE_LENGTH, QUERY_CHUNK):
                columns = slice(first, first + QUERY_CHUNK)
                q, d = q_ref[rows, columns], d_ref[rows, columns]
                delta = jnp.sum(
                    d.astype(F32) * mixed_ref[rows, columns].astype(F32), 0, keepdims=True
                )
                scores = product(keys, q) * scale
                weights = jnp.exp2(scores - sum_ref[head : head + 1, columns])
                weights = jnp.where(visible(prefix, first), weights, 0.0)
                dweights = product(values, d)
                dscores = (weights * (dweights - delta)).astype(BF16)
                dvalues = dvalues + product(weights.astype(BF16), d.T)
                dkeys = dkeys + product(dscores, q.T)
                dq = product(keys_flat, dscores) * SCORE_SCALE
                dq_ref[rows, columns] = rotate(
                    dq, cosine[:, columns], sine[:, columns], -1.0
                ).astype(BF16)
        dk_ref[...] = rotate((dkeys * SCORE_SCALE).T, cosine, sine, -1.0).astype(BF16)
        dv_ref[...] = dvalues.T.astype(BF16)

    slim = pl.BlockSpec((HEAD_WIDTH, SEQUENCE_LENGTH), lambda s, j: (j, s))
    table = whole((HEAD_WIDTH // 2, SEQUENCE_LENGTH))
    q_features, kv_features = features // 2, features // 4
    return Phase(
        body,
        (tokens // SEQUENCE_LENGTH, kv_heads),
        [query, key, value, query, query, sums, table, table],
        [query, slim, slim],
        [Name.qkv, Name.qkv, Name.qkv, Name.dmixed, Name.mixed, Name.logsums, Name.cosine, Name.sine],
        [
            (Name.dqkv, pl.ds(0, q_features)),
            (Name.dqkv, pl.ds(q_features, kv_features)),
            (Name.dqkv, pl.ds(q_features + kv_features, kv_features)),
        ],
        **timing,
    )


def attention_out_phase(tokens, width, full_shape, **timing):
    block = 256
    features = full_shape[-1]

    def body(refs, index, mixed_ref, w_ref):
        exchange = Exchange(refs)
        rows = pl.ds(pl.multiple_of(index[0] * block, block), block)
        value = product(mixed_ref[...], w_ref[...].reshape(width, features), 0, 1)
        exchange.own[rows, :] = value.astype(BF16)
        exchange.copy(index[0], rows, pl.ds(0, width)).start()

    return Phase(
        body,
        (tokens // block,),
        [pl.BlockSpec((features, block), lambda i: (0, i)), whole(full_shape)],
        [],
        [Name.mixed, Name.o_full],
        [],
        **timing,
    )


def received(refs, index, tokens, width, wide):
    block = 256
    exchange = Exchange(refs)
    rows = pl.ds(pl.multiple_of(index * block, block), block)
    for part in range(width // wide):
        copy = exchange.copy(part * (tokens // block) + index, rows, pl.ds(part * wide, wide))
        copy.wait_recv()
        copy.wait_send()
    return exchange.own[rows, :].astype(F32) + exchange.other[rows, :].astype(F32)


def row_blocks(width):
    return pl.BlockSpec((256, width), lambda i: (i, 0))


def second_norm_phase(tokens, width, **timing):
    def body(refs, index, x_ref, middle_ref, n_ref):
        attn = received(refs, index[0], tokens, width, width)
        middle = x_ref[...].astype(F32) + attn
        middle_ref[...] = middle.astype(BF16)
        n_ref[...] = (middle * row_scale(middle) * refs[Name.gains][1:]).astype(BF16)

    rows = row_blocks(width)
    return Phase(
        body,
        (tokens // 256,),
        [rows],
        [rows, rows],
        [Name.block_in],
        [Name.middle, Name.normed_two],
        **timing,
    )


def feed_forward_phase(tokens, lead, units, **timing):
    tall, wide = 1024, 512
    width = math.prod(lead)

    def body(refs, index, n_ref, gate_w, up_w, gate_ref, up_ref, hidden_ref):
        normed = n_ref[...]
        gate = product(normed, gate_w[...].reshape(width, wide))
        up = product(normed, up_w[...].reshape(width, wide))
        gate_ref[...] = gate.astype(BF16)
        up_ref[...] = up.astype(BF16)
        hidden_ref[...] = (gate * jax.nn.sigmoid(gate) * up).astype(BF16)

    weight = pl.BlockSpec(lead + (wide,), lambda j, i: (0, 0, 0, 0, j))
    out = pl.BlockSpec((tall, wide), lambda j, i: (i, j))
    return Phase(
        body,
        (units // wide, tokens // tall),
        [pl.BlockSpec((tall, width), lambda j, i: (i, 0)), weight, weight],
        [out, out, out],
        [Name.normed_two, Name.gate_full, Name.up_full],
        [Name.gate, Name.up, Name.hidden],
        **timing,
    )


def feed_backward_phase(tokens, width, units, **timing):
    tall, wide = 1024, 256

    def body(refs, index, d_ref, down_w, gate_ref, up_ref, dgate_ref, dup_ref):
        dhidden = product(d_ref[...], down_w[...])
        gate = gate_ref[...].astype(F32)
        sigmoid = jax.nn.sigmoid(gate)
        dup_ref[...] = (dhidden * gate * sigmoid).astype(BF16)
        dgate_ref[...] = (
            dhidden * up_ref[...].astype(F32) * sigmoid * (1.0 + gate * (1.0 - sigmoid))
        ).astype(BF16)

    tile = pl.BlockSpec((tall, wide), lambda i, j: (i, j))
    return Phase(
        body,
        (tokens // tall, units // wide),
        [
            pl.BlockSpec((tall, width), lambda i, j: (i, 0)),
            pl.BlockSpec((width, wide), lambda i, j: (0, j)),
            tile,
            tile,
        ],
        [tile, tile],
        [Name.out_grad, Name.down_full, Name.gate, Name.up],
        [Name.dgate, Name.dup],
        **timing,
    )


def weight_grad_phase(tokens, lead, columns, inputs, output, wide, flat=False, **timing):
    tiles = 2
    tall = math.prod(lead) // tiles

    def body(refs, index, left_ref, right_ref, out_ref):
        value = product(left_ref[...], right_ref[...], 0, 1 if flat else 0)
        out_ref[...] = value.astype(BF16).reshape(out_ref.shape)

    right = (
        pl.BlockSpec((wide, tokens), lambda i, j: (j, 0))
        if flat
        else pl.BlockSpec((tokens, wide), lambda i, j: (0, j))
    )
    out = pl.BlockSpec((lead[0] // tiles,) + lead[1:] + (wide,), lambda i, j: (i, 0, 0, 0, j))
    return Phase(
        body,
        (tiles, columns // wide),
        [pl.BlockSpec((tokens, tall), lambda i, j: (0, i)), right],
        [out],
        inputs,
        [output],
        **timing,
    )


def partial_rows_phase(tokens, width, terms, **timing):
    block, wide = 256, PARTIAL_COLUMNS

    def body(refs, index, *blocks):
        exchange = Exchange(refs)
        value = 0.0
        for number, (_, _, depth, flat) in enumerate(terms):
            left, right = blocks[2 * number : 2 * number + 2]
            value = value + product(left[...], right[...], 0 if flat else 1, 1)
        rows = pl.ds(pl.multiple_of(index[1] * block, block), block)
        columns = pl.ds(pl.multiple_of(index[0] * wide, wide), wide)
        exchange.own[rows, columns] = value.astype(BF16)
        exchange.copy(index[0] * (tokens // block) + index[1], rows, columns).start()

    specs, inputs = [], []
    for left, right, depth, flat in terms:
        specs.append(
            pl.BlockSpec((depth, block), lambda n, i: (0, i))
            if flat
            else pl.BlockSpec((block, depth), lambda n, i: (i, 0))
        )
        specs.append(pl.BlockSpec((wide, depth), lambda n, i: (n, 0)))
        inputs += [left, right]
    return Phase(body, (width // wide, tokens // block), specs, [], inputs, [], **timing)


def add_gain(refs, row, index, value):
    total = refs[Name.share_gain, 0]

    @pl.when(index == 0)
    def _():
        total[row : row + 1] = jnp.zeros_like(total[row : row + 1])

    total[row : row + 1] += jnp.sum(value, 0, keepdims=True)


def norm_back_phase(tokens, width, row, inputs, outputs, features=None, **timing):
    def body(refs, index, row_ref, back_ref, *others):
        dnorm = received(refs, index[0], tokens, width, PARTIAL_COLUMNS)
        values = row_ref[...].astype(F32)
        inverse = row_scale(values)
        unit = values * inverse
        add_gain(refs, row, index[0], dnorm * unit)
        change = norm_back(dnorm, refs[Name.gains][row : row + 1], unit, inverse)
        total = (back_ref[...].astype(F32) + change).astype(BF16)
        if features is None:
            others[0][...] = total
        else:
            w_ref, out_ref, mixed_ref = others
            out_ref[...] = total
            mixed_ref[...] = product(w_ref[...], total, 0, 1).astype(BF16)

    rows = row_blocks(width)
    in_specs, out_specs = [rows, rows], [rows]
    if features is not None:
        in_specs.append(whole((width, features)))
        out_specs.append(pl.BlockSpec((features, 256), lambda i: (0, i)))
    return Phase(body, (tokens // 256,), in_specs, out_specs, inputs, outputs, **timing)


def block_out_phase(tokens, width, **timing):
    def body(refs, index, middle_ref, out_ref):
        ffn = received(refs, index[0], tokens, width, PARTIAL_COLUMNS)
        out_ref[...] = (middle_ref[...].astype(F32) + ffn).astype(BF16)

    rows = row_blocks(width)
    return Phase(
        body, (tokens // 256,), [rows], [rows], [Name.middle], [Name.block_out], **timing
    )


def norm_back(dnorm, gain_row, unit_rows, inverse):
    scaled = dnorm * gain_row
    return inverse * (scaled - unit_rows * jnp.mean(scaled * unit_rows, -1, keepdims=True))


def adam_step(weight, gradient, first_moment, second_moment, rate, decay, factor, fix_one, fix_two):
    clipped = factor * gradient
    first_new = beta_one * first_moment + (1.0 - beta_one) * clipped
    second_new = beta_two * second_moment + (1.0 - beta_two) * clipped * clipped
    update = first_new / fix_one / (jnp.sqrt(second_new / fix_two) + adam_eps) + decay * weight
    return (weight - rate * update, first_new, second_new)


def local(
    block_in,
    prefix_len,
    out_grad,
    step_count,
    q_weight,
    key_matrix,
    value_matrix,
    o_weight,
    gate_weight,
    up_weight,
    down_weight,
    norm_gains,
    query_mean_moment,
    key_mean_moment,
    value_mean_moment,
    output_mean_moment,
    gate_mean_moment,
    up_mean_moment,
    down_mean_moment,
    gains_mean_moment,
    q_second,
    key_square_moment,
    value_square_moment,
    o_second,
    gate_second,
    up_second,
    down_second,
    gains_second,
):
    dims = factor(lax.axis_size("dp"))
    width = block_in.shape[1]
    q_width, kv_width = q_weight.shape[1], key_matrix.shape[1]
    units = gate_weight.shape[1]
    tokens = block_in.shape[0]
    features = q_width + 2 * kv_width
    blocks = tokens // 256
    rows = q_weight.shape[0]
    lead = dims + (rows,)
    devices = lax.axis_size("dp")
    cosine, sine = rotary_tables()
    gains = (norm_gains, pl.BlockSpec(memory_space=pltpu.VMEM))
    prefix = (prefix_len, pl.BlockSpec(memory_space=pltpu.SMEM))
    per_token = out_like(tokens, width)
    per_unit = out_like(tokens, units)

    plan = Gather(
        {
            Name.qkv_full: [q_weight, key_matrix, value_matrix],
            Name.o_full: [o_weight],
            Name.gate_full: [gate_weight],
            Name.up_full: [up_weight],
            Name.down_full: [down_weight],
        },
        dims,
        (2, 3),
    )
    first = done_row(plan, (0,))
    then = done_row(plan, (1,))
    starts = [done_row(plan, (2, 3), end) for end in range(512, units + 1, 512)]
    soon = starts[0]
    held = [mark for mark in [*starts[1:], starts[-1]] for _ in range(tokens // 1024)]
    held = [
        max(mark, len(plan.slots) - 2 - (len(held) - number) * 5 // len(held))
        for number, mark in enumerate(held, 1)
    ]
    made = chain(
        "forward",
        [
            project_phase(
                tokens, width, features, lead + (features,), before=first, until=first + 3
            ),
            attend_forward_phase(tokens, features, until=max(then, first + 8)),
            attention_out_phase(
                tokens, width, lead + (q_width,), before=then, until=max(then, first + 10)
            ),
            second_norm_phase(tokens, width, until=max(soon, first + 11)),
            feed_forward_phase(tokens, lead, units, before=soon, marks=held),
            weight_grad_phase(
                tokens,
                lead,
                units,
                [Name.out_grad, Name.hidden],
                Name.grad_down,
                1024,
                until=len(plan.slots),
            ),
        ],
        {
            Name.block_in: block_in,
            Name.cosine: cosine,
            Name.sine: sine,
            Name.out_grad: out_grad,
        },
        {Name.gains: gains, Name.prefix: prefix},
        {
            Name.normed_one: per_token,
            Name.qkv: out_like(features, tokens),
            Name.mixed: out_like(q_width, tokens),
            Name.logsums: out_like(kv_width // HEAD_WIDTH, GROUP_WIDTH, tokens, dtype=F32),
            Name.middle: per_token,
            Name.normed_two: per_token,
            Name.gate: per_unit,
            Name.up: per_unit,
            Name.hidden: per_unit,
            Name.grad_down: out_like(*lead, units),
        },
        {},
        Exchange.scratch(tokens, width, blocks),
        plan,
        0,
    )
    for name in (Name.qkv_full, Name.o_full, Name.gate_full, Name.up_full, Name.down_full):
        made[name] = made[name].reshape(width, -1)

    plan = Scatter(
        [
            (Name.grad_down, units, Name.sum_down),
            (Name.grad_gate, units, Name.sum_gate),
            (Name.grad_up, units, Name.sum_up),
            (Name.grad_out, q_width, Name.sum_out),
            (Name.grad_qkv, features, Name.sum_qkv),
        ],
        dims,
        rows,
    )
    gate_row, up_row, out_row, qkv_row = (start_row(plan, (which,)) for which in range(1, 5))
    last = len(plan.slots)

    def share_gains(refs):
        Everyone(*(refs[Name.share_gain, part] for part in range(4)), False).start()
        Exchange.release(refs)

    def share_squares(refs):
        refs[Name.gain_sum][...] = Everyone(
            *(refs[Name.share_gain, part] for part in range(4)), False
        ).finish()
        everyone = Everyone(*(refs[Name.share_square, part] for part in range(4)), True)
        everyone.message[...] = refs[Name.squares][...]
        everyone.start()
        refs[Name.square_sum][...] = everyone.finish()

    scratch = Exchange.scratch(tokens, width, blocks * (width // PARTIAL_COLUMNS))
    for part, kind in enumerate(Everyone.scratch(devices, 2, width)):
        scratch[Name.share_gain, part] = kind
    for part, kind in enumerate(
        Everyone.scratch(devices * lax.axis_size("tensor"), 1, CHUNK)
    ):
        scratch[Name.share_square, part] = kind
    kept = (
        Name.down_full,
        Name.gate,
        Name.up,
        Name.normed_two,
        Name.gate_full,
        Name.up_full,
        Name.middle,
        Name.o_full,
        Name.qkv,
        Name.mixed,
        Name.logsums,
        Name.normed_one,
        Name.qkv_full,
        Name.hidden,
        Name.grad_down,
    )
    made |= chain(
        "backward",
        [
            feed_backward_phase(tokens, width, units, until=gate_row // 2),
            weight_grad_phase(
                tokens,
                lead,
                units,
                [Name.normed_two, Name.dgate],
                Name.grad_gate,
                512,
                until=gate_row,
            ),
            weight_grad_phase(
                tokens,
                lead,
                units,
                [Name.normed_two, Name.dup],
                Name.grad_up,
                512,
                until=min(up_row, gate_row + 2),
            ),
            partial_rows_phase(
                tokens,
                width,
                [
                    (Name.dgate, Name.gate_full, units, False),
                    (Name.dup, Name.up_full, units, False),
                ],
                until=gate_row + 6,
            ),
            norm_back_phase(
                tokens,
                width,
                1,
                [Name.middle, Name.out_grad, Name.o_full],
                [Name.dmiddle, Name.dmixed],
                q_width,
                until=gate_row + 8,
                after=Exchange.release,
            ),
            weight_grad_phase(
                tokens,
                lead,
                q_width,
                [Name.dmiddle, Name.mixed],
                Name.grad_out,
                q_width,
                flat=True,
                until=out_row,
            ),
            attend_backward_phase(tokens, features, until=qkv_row),
            weight_grad_phase(
                tokens, lead, features, [Name.normed_one, Name.dqkv], Name.grad_qkv, 768, flat=True
            ),
            partial_rows_phase(
                tokens,
                width,
                [(Name.dqkv, Name.qkv_full, features, True)],
                until=qkv_row + 3,
                enter=Exchange.claim,
            ),
            norm_back_phase(
                tokens,
                width,
                0,
                [Name.block_in, Name.dmiddle],
                [Name.in_grad],
                until=qkv_row + 4,
                after=share_gains,
            ),
            partial_rows_phase(
                tokens,
                width,
                [(Name.hidden, Name.down_full, units, False)],
                until=qkv_row + 7,
                enter=Exchange.claim,
            ),
            block_out_phase(tokens, width, until=qkv_row + 8),
        ],
        {
            Name.out_grad: out_grad,
            Name.block_in: block_in,
            Name.cosine: cosine,
            Name.sine: sine,
        }
        | {name: made[name] for name in kept},
        {Name.gains: gains, Name.prefix: prefix},
        {
            Name.dgate: per_unit,
            Name.dup: per_unit,
            Name.grad_gate: out_like(*lead, units),
            Name.grad_up: out_like(*lead, units),
            Name.dmiddle: per_token,
            Name.dmixed: out_like(q_width, tokens),
            Name.grad_out: out_like(*lead, q_width),
            Name.dqkv: out_like(features, tokens),
            Name.grad_qkv: out_like(*lead, features),
            Name.in_grad: per_token,
            Name.block_out: per_token,
        },
        {
            Name.gain_sum: out_like(2, width, dtype=F32),
            Name.square_sum: out_like(1, CHUNK, dtype=F32),
        },
        scratch,
        plan,
        1,
        share_squares,
    )
    sum_qkv, sum_out, sum_gate, sum_up, sum_down = (
        made[name]
        for name in (Name.sum_qkv, Name.sum_out, Name.sum_gate, Name.sum_up, Name.sum_down)
    )
    block_out = made[Name.block_out]
    in_grad = made[Name.in_grad].astype(F32)
    gain_sum = made[Name.gain_sum]
    total_square = jnp.sum(made[Name.square_sum]) + jnp.sum(jnp.square(gain_sum))
    gain_width = width // devices
    first_column = lax.axis_index("dp") * gain_width
    grad_gains = lax.dynamic_slice_in_dim(gain_sum, first_column, gain_width, 1)
    old_gains = lax.dynamic_slice_in_dim(norm_gains, first_column, gain_width, 1)
    reduced = (
        sum_qkv[:, :q_width],
        sum_qkv[:, q_width : q_width + kv_width],
        sum_qkv[:, q_width + kv_width :],
        sum_out,
        sum_gate,
        sum_up,
        sum_down,
        grad_gains,
    )
    grad_norm = jnp.sqrt(total_square)
    factor_now = jnp.minimum(1.0, clip_limit / grad_norm)
    step_float = step_count[0].astype(F32)
    fix_one = 1.0 - jnp.power(beta_one, step_float)
    fix_two = 1.0 - jnp.power(beta_two, step_float)
    masters = (
        q_weight,
        key_matrix,
        value_matrix,
        o_weight,
        gate_weight,
        up_weight,
        down_weight,
        old_gains,
    )
    firsts = (
        query_mean_moment,
        key_mean_moment,
        value_mean_moment,
        output_mean_moment,
        gate_mean_moment,
        up_mean_moment,
        down_mean_moment,
        gains_mean_moment,
    )
    seconds = (
        q_second,
        key_square_moment,
        value_square_moment,
        o_second,
        gate_second,
        up_second,
        down_second,
        gains_second,
    )
    rate_list = matrix_rates + (gain_rate,)
    decay_list = (decay_rate,) * 7 + (0.0,)
    new_weights, new_firsts, new_seconds = ([], [], [])
    for weight, gradient, first_moment, second_moment, rate, decay in zip(
        masters, reduced, firsts, seconds, rate_list, decay_list
    ):
        weight_new, first_new, second_new = adam_step(
            weight, gradient, first_moment, second_moment, rate, decay, factor_now, fix_one, fix_two
        )
        new_weights.append(weight_new)
        new_firsts.append(first_new)
        new_seconds.append(second_new)
    return (
        block_out,
        in_grad,
        grad_norm.reshape(1),
        new_weights[0],
        new_weights[1],
        new_weights[2],
        new_weights[3],
        new_weights[4],
        new_weights[5],
        new_weights[6],
        new_weights[7],
        new_firsts[0],
        new_firsts[1],
        new_firsts[2],
        new_firsts[3],
        new_firsts[4],
        new_firsts[5],
        new_firsts[6],
        new_firsts[7],
        new_seconds[0],
        new_seconds[1],
        new_seconds[2],
        new_seconds[3],
        new_seconds[4],
        new_seconds[5],
        new_seconds[6],
        new_seconds[7],
    )


def solution(mesh):
    return jax.shard_map(
        local,
        mesh=mesh,
        in_specs=(
            P("dp", None),
            P("dp"),
            P("dp", None),
            P(),
            P("dp", "tensor"),
            P("dp", "tensor"),
            P("dp", "tensor"),
            P("dp", "tensor"),
            P("dp", "tensor"),
            P("dp", "tensor"),
            P("dp", "tensor"),
            P(),
            P("dp", "tensor"),
            P("dp", "tensor"),
            P("dp", "tensor"),
            P("dp", "tensor"),
            P("dp", "tensor"),
            P("dp", "tensor"),
            P("dp", "tensor"),
            P(None, "dp"),
            P("dp", "tensor"),
            P("dp", "tensor"),
            P("dp", "tensor"),
            P("dp", "tensor"),
            P("dp", "tensor"),
            P("dp", "tensor"),
            P("dp", "tensor"),
            P(None, "dp"),
        ),
        out_specs=(
            P("dp", None),
            P("dp", None),
            P(),
            P("dp", "tensor"),
            P("dp", "tensor"),
            P("dp", "tensor"),
            P("dp", "tensor"),
            P("dp", "tensor"),
            P("dp", "tensor"),
            P("dp", "tensor"),
            P(None, "dp"),
            P("dp", "tensor"),
            P("dp", "tensor"),
            P("dp", "tensor"),
            P("dp", "tensor"),
            P("dp", "tensor"),
            P("dp", "tensor"),
            P("dp", "tensor"),
            P(None, "dp"),
            P("dp", "tensor"),
            P("dp", "tensor"),
            P("dp", "tensor"),
            P("dp", "tensor"),
            P("dp", "tensor"),
            P("dp", "tensor"),
            P("dp", "tensor"),
            P(None, "dp"),
        ),
        check_vma=False,
    )
```
